32 devices in a mesh: seq: 8 (over z, y), ch: 4 (over x, core).
Axes of the slice: x: 2, y: 2, z: 4, core: 2. Of those that a mesh axis runs over, the one named last changes fastest.
Arguments:
- inputs: bfloat16 [1024, 4096], P('seq', 'ch'), may hold values from -6 to 6
- gate_values: bfloat16 [1024, 4096], P('seq', 'ch'), may hold values from -6 to 6
- grad_out: bfloat16 [1024, 4096], P('seq', 'ch'), may hold values from -6 to 6
- first_weight: float32 [32, 256], replicated, may hold values from -4 to 4
- first_bias: float32 [256], replicated, may hold values from -3.140625 to 3.140625
- second_weight: float32 [256, 256], replicated, may hold values from -0.75 to 0.75
- second_bias: float32 [256], replicated, may hold values from -3.140625 to 3.140625
- out_weight: float32 [256, 4096], P(None, 'ch'), may hold values from -0.0546875 to 0.0546875
- decay_rates: float32 [4096], P('ch'), as said below
- mask_lengths: int32 [4096], P('ch'), may hold values from 1 to 512, as said below
Outputs:
- grad_inputs: bfloat16 [1024, 4096], P('seq', 'ch')
- grad_gates: bfloat16 [1024, 4096], P('seq', 'ch')
- grad_first_weight: float32 [32, 256], replicated
- grad_first_bias: float32 [256], replicated
- grad_second_weight: float32 [256, 256], replicated
- grad_second_bias: float32 [256], replicated
- grad_out_weight: float32 [256, 4096], P(None, 'ch')
The draws below stay inside these ranges and needn't reach their ends.
Inputs may be any that keep to these rules, and one draw needn't show every extreme that they name: `mask_lengths`: each channel's decay-mask length in lags; in every aligned group of 32 channels at least one channel has exactly 512. `decay_rates`: positive decay rates between 1 / 5120 and 1 / 40.
All inputs are finite; a program needn't handle non-finite values.
Results may differ from the reference program's by a relative error of at most 0.013.
Values may be sent and summed in bfloat16 or wider, within the bound.
A program may use at most 128 MiB of HBM per device.

```python
import math
import jax
import jax.numpy as jnp
from jax import lax

D = 4096
FW = 256
EMB = 32
WIN = 512
TOKENS = 1024


def draw_decay_rates(key, part):
    key_slow = jax.random.fold_in(key, 0)
    lowest = math.log(0.1 / WIN)
    highest = math.log(1.0 / 40.0)
    spread = jax.random.uniform(key_slow, (D,), jnp.float32, lowest, highest)
    return jnp.exp(spread).astype(jnp.float32)


def draw_mask_lengths(key, part):
    key_base, key_spot = jax.random.split(key)
    base_lengths = jax.random.randint(key_base, (D,), 1, WIN + 1, dtype=jnp.int32)
    groups = D // 32
    chosen_slot = jax.random.randint(key_spot, (groups, 1), 0, 32, dtype=jnp.int32)
    hitting = jnp.arange(32, dtype=jnp.int32)[None, :] == chosen_slot
    return jnp.where(hitting.reshape(D), WIN, base_lengths).astype(jnp.int32)


def levels(key, dims, pieces, low, largest):
    def one(axis_at, blocks):
        steps = jax.random.uniform(jax.random.fold_in(jax.random.fold_in(key, 6), axis_at), (blocks,), jnp.float32, low / len(pieces), largest / len(pieces))
        return jnp.repeat(jnp.exp(steps), dims[axis_at] // blocks).reshape((-1,) + (1,) * (len(dims) - axis_at - 1))

    level = one(*pieces[0])
    for cut in pieces[1:]:
        level = level * one(*cut)
    return level


def bell_draw(stream_key, dims, scale, reach, cuts=(), kind=jnp.bfloat16):
    gain = levels(stream_key, dims, cuts, -0.22, 0.18) if cuts else 1.0
    drawn = jax.random.normal(stream_key, dims, jnp.float32) * scale * gain
    return jnp.minimum(jnp.maximum(drawn, -reach), reach).astype(kind)


def setup_inputs(seed: int = 0) -> dict:
    splits = jax.random.split(jax.random.key(seed), 11)
    return {
        "inputs": bell_draw(splits[0], (TOKENS, D), 1.0, 6.0, ((0, 8), (1, 4))),
        "gate_values": bell_draw(splits[1], (TOKENS, D), 1.0, 6.0, ((0, 8), (1, 4))),
        "grad_out": bell_draw(splits[2], (TOKENS, D), 1.0, 6.0, ((0, 8), (1, 4))),
        "first_weight": bell_draw(splits[3], (EMB, FW), 1.0, 4.0, (), jnp.float32),
        "first_bias": jnp.clip(jax.random.uniform(splits[4], (FW,), jnp.float32, -3.140625, 3.140625), -3.140625, 3.140625),
        "second_weight": bell_draw(splits[5], (FW, FW), (FW // 4) ** -0.5, 0.75, (), jnp.float32),
        "second_bias": jnp.clip(jax.random.uniform(splits[6], (FW,), jnp.float32, -3.140625, 3.140625), -3.140625, 3.140625),
        "out_weight": bell_draw(splits[7], (FW, D), (FW * WIN // 10) ** -0.5, 0.0546875, ((1, 4),), jnp.float32),
        "decay_rates": draw_decay_rates(jax.random.fold_in(splits[10], 71), 0),
        "mask_lengths": draw_mask_lengths(jax.random.fold_in(splits[10], 71), 0),
    }


FULL_PRECISION = lax.Precision.HIGHEST

def angle_table(first_index, second_index, period):
    product = first_index[:, None] * second_index[None, :] % period
    return 2.0 * math.pi / period * product.astype(jnp.float32)

def lag_features(lag_count, feature_count):
    lag_index = jnp.arange(lag_count, dtype=jnp.int32)
    band_index = jnp.arange(feature_count // 2, dtype=jnp.int32) + 1
    phases = angle_table(lag_index, band_index, 2 * feature_count)
    return jnp.concatenate([jnp.cos(phases), jnp.sin(phases)], axis=1)

def reference(inputs, gate_values, grad_out, first_weight, first_bias, second_weight, second_bias, out_weight, decay_rates, mask_lengths):
    features = lag_features(WIN, EMB)
    pre_first = jnp.dot(features, first_weight, precision=FULL_PRECISION) + first_bias
    hidden_one = jnp.sin(pre_first)
    pre_second = jnp.dot(hidden_one, second_weight, precision=FULL_PRECISION) + second_bias
    hidden_two = jnp.sin(pre_second)
    lag_index = jnp.arange(WIN, dtype=jnp.int32)
    envelope = jnp.exp(-decay_rates[None, :] * lag_index.astype(jnp.float32)[:, None]) * (lag_index[:, None] < mask_lengths[None, :]).astype(jnp.float32)
    filter_taps = jnp.dot(hidden_two, out_weight, precision=FULL_PRECISION) * envelope
    padded_taps = jnp.pad(filter_taps, ((0, TOKENS - WIN), (0, 0)))
    taps_spectrum = jnp.fft.rfft(padded_taps, axis=0)
    input_spectrum = jnp.fft.rfft(inputs.astype(jnp.float32), axis=0)
    convolved = jnp.fft.irfft(taps_spectrum * input_spectrum, n=TOKENS, axis=0).astype(jnp.float32)
    grad_gates = (grad_out.astype(jnp.float32) * convolved).astype(jnp.bfloat16)
    carried = (grad_out.astype(jnp.float32) * gate_values.astype(jnp.float32)).astype(jnp.bfloat16)
    carried = lax.optimization_barrier(carried).astype(jnp.float32)
    carried_spectrum = jnp.fft.rfft(carried, axis=0)
    grad_inputs = jnp.fft.irfft(jnp.conj(taps_spectrum) * carried_spectrum, n=TOKENS, axis=0).astype(jnp.float32).astype(jnp.bfloat16)
    tap_sums = jnp.fft.irfft(carried_spectrum * jnp.conj(input_spectrum), n=TOKENS, axis=0)[:WIN].astype(jnp.float32)
    grad_taps = tap_sums * envelope * (1.0 / math.sqrt(TOKENS * WIN))
    grad_out_weight = jnp.dot(hidden_two.T, grad_taps, precision=FULL_PRECISION)
    grad_two = jnp.dot(grad_taps, out_weight.T, precision=FULL_PRECISION) * jnp.cos(pre_second)
    grad_second_weight = jnp.dot(hidden_one.T, grad_two, precision=FULL_PRECISION)
    grad_second_bias = lax.optimization_barrier(jnp.sum(grad_two, axis=0))
    grad_one = jnp.dot(grad_two, second_weight.T, precision=FULL_PRECISION) * jnp.cos(pre_first)
    grad_first_weight = jnp.dot(features.T, grad_one, precision=FULL_PRECISION)
    grad_first_bias = lax.optimization_barrier(jnp.sum(grad_one, axis=0))
    return (grad_inputs, grad_gates, grad_first_weight, grad_first_bias, grad_second_weight, grad_second_bias, grad_out_weight)
```

```python
import math

import jax
import jax.numpy as jnp
import functools

import numpy as np
from jax import lax
from jax.experimental import pallas as pl
from jax.experimental.pallas import tpu as pltpu
from jax.sharding import PartitionSpec as P

SPAN = 4


FULL_PRECISION = lax.Precision.HIGHEST


def passed_along(value, axis, steps):
    count = lax.axis_size(axis)
    pairs = [(source, (source + steps) % count) for source in range(count)]
    return lax.ppermute(value, axis, pairs)


def angle_table(first_index, second_index, period):
    product = first_index[:, None] * second_index[None, :] % period
    return 2.0 * math.pi / period * product.astype(jnp.float32)


def lag_features(lag_count, feature_count):
    lag_index = jnp.arange(lag_count, dtype=jnp.int32)
    band_index = jnp.arange(feature_count // 2, dtype=jnp.int32) + 1
    phases = angle_table(lag_index, band_index, 2 * feature_count)
    return jnp.concatenate([jnp.cos(phases), jnp.sin(phases)], axis=1)


def split_table(table):
    upper_part = table.astype(jnp.bfloat16)
    lower_part = (table - upper_part.astype(jnp.float32)).astype(jnp.bfloat16)
    return (upper_part, lower_part)


def transform_tables(shard_rows):
    period = 2 * shard_rows
    frequency = jnp.arange(shard_rows + 1, dtype=jnp.int32)
    position = jnp.arange(shard_rows, dtype=jnp.int32)
    bin_weight = jnp.where((frequency == 0) | (frequency == shard_rows), 1.0, 2.0).astype(
        jnp.float32
    )
    forward_angles = angle_table(frequency, position, period)
    mirror_angles = angle_table(frequency, shard_rows - 1 - position, period)
    back_angles = angle_table(position + shard_rows, frequency, period)
    mirror_back = angle_table(2 * shard_rows - 1 - position, frequency, period)
    front_table = jnp.stack([jnp.cos(forward_angles), -jnp.sin(forward_angles)])
    mirror_table = jnp.stack([jnp.cos(mirror_angles), -jnp.sin(mirror_angles)])
    back_plain = jnp.stack([jnp.cos(back_angles), -jnp.sin(back_angles)]) / period
    back_table = back_plain * bin_weight[None, None, :]
    mirror_out = jnp.stack([jnp.cos(mirror_back), -jnp.sin(mirror_back)]) * (
        bin_weight[None, None, :] / period
    )
    fold_table = front_table * bin_weight[None, :, None]
    parity = (1.0 - 2.0 * (frequency % 2).astype(jnp.float32))[None, :, None]
    return (front_table, mirror_table, back_plain, back_table, mirror_out, fold_table, parity)


def spectrum(table_in, signal):
    return jnp.einsum("kfs,sc->kfc", table_in, signal, precision=FULL_PRECISION)


def sample_spectrum(table_pair, signal):
    upper_term = jnp.einsum(
        "kfs,sc->kfc", table_pair[0], signal, preferred_element_type=jnp.float32
    )
    lower_term = jnp.einsum(
        "kfs,sc->kfc", table_pair[1], signal, preferred_element_type=jnp.float32
    )
    return upper_term + lower_term


def sample_pullback(table_pair, signal):
    upper_term = jnp.einsum(
        "ksf,sc->kfc", table_pair[0], signal, preferred_element_type=jnp.float32
    )
    lower_term = jnp.einsum(
        "ksf,sc->kfc", table_pair[1], signal, preferred_element_type=jnp.float32
    )
    return upper_term + lower_term


def complex_product(left_factor, right_factor):
    real_part = left_factor[0] * right_factor[0] - left_factor[1] * right_factor[1]
    imag_part = left_factor[0] * right_factor[1] + left_factor[1] * right_factor[0]
    return jnp.stack([real_part, imag_part])


def conjugate_product(left_factor, right_factor):
    real_part = left_factor[0] * right_factor[0] + left_factor[1] * right_factor[1]
    imag_part = left_factor[1] * right_factor[0] - left_factor[0] * right_factor[1]
    return jnp.stack([real_part, imag_part])


def weighted_sum(filter_mixes, spectra_items):
    accumulated = complex_product(filter_mixes[0], spectra_items[0])
    for offset in range(1, len(filter_mixes)):
        accumulated = accumulated + complex_product(filter_mixes[offset], spectra_items[offset])
    return accumulated


def per_device(
    inputs,
    gate_values,
    grad_out,
    first_weight,
    first_bias,
    second_weight,
    second_bias,
    out_weight,
    decay_rates,
    mask_lengths,
):
    shard_rows = inputs.shape[0]
    window = SPAN * shard_rows
    front_table, mirror_table, back_plain, back_table, mirror_out, fold_table, parity = (
        transform_tables(shard_rows)
    )
    front_pair = split_table(front_table)
    mirror_pair = split_table(mirror_table)
    pull_pair = split_table(back_plain)
    features = lag_features(window, first_weight.shape[0])
    pre_first = jnp.dot(features, first_weight, precision=FULL_PRECISION) + first_bias
    hidden_one = jnp.sin(pre_first)
    pre_second = jnp.dot(hidden_one, second_weight, precision=FULL_PRECISION) + second_bias
    hidden_two = jnp.sin(pre_second)
    lag_index = jnp.arange(window, dtype=jnp.int32)
    envelope = jnp.exp(-decay_rates[None, :] * lag_index.astype(jnp.float32)[:, None]) * (
        lag_index[:, None] < mask_lengths[None, :]
    ).astype(jnp.float32)
    filter_taps = jnp.dot(hidden_two, out_weight, precision=FULL_PRECISION) * envelope
    block_spectra = [
        spectrum(front_table, filter_taps[block * shard_rows : (block + 1) * shard_rows])
        for block in range(SPAN)
    ]
    filter_mixes = []
    for offset in range(SPAN + 1):
        if offset == 0:
            mixed = parity * block_spectra[0]
        elif offset == SPAN:
            mixed = block_spectra[SPAN - 1]
        else:
            mixed = block_spectra[offset - 1] + parity * block_spectra[offset]
        filter_mixes.append(mixed)
    carried = (grad_out.astype(jnp.float32) * gate_values.astype(jnp.float32)).astype(jnp.bfloat16)
    earlier_spectra = [sample_spectrum(front_pair, inputs)]
    later_spectra = [sample_spectrum(mirror_pair, carried)]
    for offset in range(1, SPAN + 1):
        earlier = passed_along(inputs, "seq", offset)
        later = passed_along(carried, "seq", -offset)
        earlier_spectra.append(sample_spectrum(front_pair, earlier))
        later_spectra.append(sample_spectrum(mirror_pair, later))
    convolved = jnp.einsum(
        "ksf,kfc->sc",
        back_table,
        weighted_sum(filter_mixes, earlier_spectra),
        precision=FULL_PRECISION,
    )
    grad_gates = (grad_out.astype(jnp.float32) * convolved).astype(jnp.bfloat16)
    grad_inputs = jnp.einsum(
        "ksf,kfc->sc",
        mirror_out,
        weighted_sum(filter_mixes, later_spectra),
        precision=FULL_PRECISION,
    ).astype(jnp.bfloat16)
    pulled = sample_pullback(pull_pair, carried)
    grad_mixes = [conjugate_product(pulled, spectra_item) for spectra_item in earlier_spectra]
    pieces = []
    for block in range(SPAN):
        grad_block = parity * grad_mixes[block] + grad_mixes[block + 1]
        pieces.append(jnp.einsum("kfs,kfc->sc", fold_table, grad_block, precision=FULL_PRECISION))
    tap_terms = jnp.concatenate(pieces, axis=0)
    grad_scale = 1.0 / math.sqrt(lax.axis_size("seq") * shard_rows * window)
    tap_sums = lax.psum(tap_terms, "seq")
    grad_taps = tap_sums * envelope * grad_scale
    grad_out_weight = jnp.dot(hidden_two.T, grad_taps, precision=FULL_PRECISION)
    unit_grad = lax.psum(
        jnp.dot(grad_taps, out_weight.T, precision=FULL_PRECISION).astype(jnp.bfloat16), "ch"
    ).astype(jnp.float32)
    grad_two = unit_grad * jnp.cos(pre_second)
    grad_second_weight = jnp.dot(hidden_one.T, grad_two, precision=FULL_PRECISION)
    grad_second_bias = jnp.sum(grad_two, axis=0)
    grad_one = jnp.dot(grad_two, second_weight.T, precision=FULL_PRECISION) * jnp.cos(pre_first)
    grad_first_weight = jnp.dot(features.T, grad_one, precision=FULL_PRECISION)
    grad_first_bias = jnp.sum(grad_one, axis=0)
    return (
        grad_inputs,
        grad_gates,
        grad_first_weight,
        grad_first_bias,
        grad_second_weight,
        grad_second_bias,
        grad_out_weight,
    )


VMEM_LIMIT = 40_000_000
DRAIN_LIMIT = 8_000_000
MESH = pl.DeviceIdType.MESH


def bf(value):
    return value.astype(jnp.bfloat16)


def dot(left, right, dims=((1,), (0,)), precision=None):
    return lax.dot_general(
        left, right, (dims, ((), ())), precision=precision, preferred_element_type=jnp.float32
    )


def packed_table(tokens):
    half = tokens // 2
    freq = np.arange(half)[:, None]
    time = np.arange(tokens)[None, :]
    angles = 2.0 * np.pi / tokens * (freq * time % tokens)
    lower = -np.sin(angles)
    lower[0] = 1.0 - 2.0 * (np.arange(tokens) % 2)
    return np.concatenate([np.cos(angles), lower]).astype(np.float32)


def exchange_kernel(
    sizes, x_hbm, gate_hbm, gout_hbm, w1_hbm, b1_hbm, w2_hbm, b2_hbm, decay_hbm, mask_hbm,
    feat_hbm, featt_hbm, ow_hbm, table_hbm, turned_hbm,
    gi_ref, gg_ref, gw1_ref, gb1_ref, gw2_ref, gb2_ref, gow_ref,
    gate_ref, gout_ref, w1_ref, b1_ref, w2_ref, b2_ref, decay_ref, mask_ref,
    feat_ref, featt_ref, ow, table, turned,
    ow_hi, ow_lo, carried, xs, cs, conv_in, taps, env, xspec, cspec, tspec, prod_v, prod_t,
    prod_g, back_v, back_g, sums, gts, gtall, units, send_sem, recv_sem, usend, urecv,
    local_sem,
):
    n, m, rows, width, window, period = sizes
    tokens = n * rows
    half = tokens // 2
    side = n // 2
    me = lax.axis_index("seq")
    mine = lax.axis_index("ch")
    steps = range(1, n)
    peers = {step: lax.rem(me + step, n) for step in steps}
    others = {step: lax.rem(mine + step, m) for step in range(1, m)}
    base_peer = me // side * side
    near = {step: base_peer + lax.rem(me - base_peer + step, side) for step in range(1, side)}
    across = lax.rem(me + side, n)

    barrier = pltpu.get_barrier_semaphore()
    for step in reversed(steps):
        pl.semaphore_signal(barrier, inc=1, device_id={"seq": peers[step]}, device_id_type=MESH)
    for step in range(1, m):
        pl.semaphore_signal(barrier, inc=1, device_id={"ch": others[step]}, device_id_type=MESH)

    own_rows = pl.ds(pl.multiple_of(me * rows, rows), rows)
    own_cols = pl.ds(pl.multiple_of(me * width, width), width)
    loads = []
    for at, (source, target) in enumerate((
        (gate_hbm, gate_ref), (gout_hbm, gout_ref), (x_hbm.at[:, own_cols], xs.at[own_rows, :]),
        (w1_hbm, w1_ref), (b1_hbm, b1_ref), (w2_hbm, w2_ref), (b2_hbm, b2_ref),
        (decay_hbm, decay_ref), (mask_hbm, mask_ref), (feat_hbm, feat_ref),
        (featt_hbm, featt_ref), (ow_hbm, ow), (table_hbm, table), (turned_hbm, turned),
    )):
        load = pltpu.make_async_copy(source, target, local_sem.at[at])
        load.start()
        loads.append(load)
    pl.semaphore_wait(barrier, n + m - 2)

    def send(kind, step, peer, source, target):
        copy = pltpu.make_async_remote_copy(
            src_ref=source, dst_ref=target,
            send_sem=send_sem.at[kind, step], recv_sem=recv_sem.at[kind, step],
            device_id={"seq": peer}, device_id_type=MESH,
        )
        copy.start()
        return copy

    def columns(step):
        return pl.ds(pl.multiple_of(peers[step] * width, width), width)

    def block(step):
        return pl.ds(pl.multiple_of(peers[step] * rows, rows), rows)

    x_moves = [
        send(0, step, peers[step], x_hbm.at[:, columns(step)], xs.at[own_rows, :])
        for step in steps
    ]
    for load in loads[:2]:
        load.wait()
    carried[...] = bf(gout_ref[...].astype(jnp.float32) * gate_ref[...].astype(jnp.float32))
    c_moves = [
        send(1, step, peers[step], carried.at[:, columns(step)], cs.at[own_rows, :])
        for step in steps
    ]
    cs[own_rows, :] = carried[:, own_cols]

    full = lax.Precision.HIGHEST
    for load in loads[2:]:
        load.wait()
    pre_one = dot(feat_ref[...], w1_ref[...], precision=full) + b1_ref[...]
    h_one = jnp.sin(pre_one)
    slope_one = jnp.cos(pre_one)
    pre_two = dot(h_one, w2_ref[...], precision=full) + b2_ref[...]
    h_two = jnp.sin(pre_two)
    slope_two = jnp.cos(pre_two)
    base = dot(h_two, ow[:, own_cols], precision=full)
    decay = decay_ref[:, own_cols]
    lengths = mask_ref[:, own_cols]
    for at in range(window // period):
        lag = lax.broadcasted_iota(jnp.int32, (period, width), 0) + at * period
        part = jnp.where(lag < lengths, jnp.exp(-decay * lag.astype(jnp.float32)), 0.0)
        env[pl.ds(at * period, period), :] = part
        taps[pl.ds(at * period, period), :] = bf(base * part)

    @pl.loop(0, tokens // 256)
    def _(i):
        piece = pl.ds(pl.multiple_of(i * 256, 256), 256)
        tspec[piece, :] = dot(table[piece, 0:window], taps[...])

    h_one_t = h_one.T
    upper_ow = bf(ow[...])
    ow_hi[...] = upper_ow
    ow_lo[...] = bf(ow[...] - upper_ow.astype(jnp.float32))
    h_two_t = bf(h_two.T)

    def parts(i):
        upper = pl.ds(pl.multiple_of(i * 64, 64), 64)
        lower = pl.ds(pl.multiple_of(half + i * 64, 64), 64)
        first = (lax.broadcasted_iota(jnp.int32, (64, width), 0) + i * 64) == 0
        weight = jnp.where(first, 1.0 / tokens, 2.0 / tokens)
        return upper, lower, first, weight

    for copy in x_moves:
        copy.wait_recv()

    @pl.loop(0, tokens // 256)
    def _(i):
        piece = pl.ds(pl.multiple_of(i * 256, 256), 256)
        xspec[piece, :] = dot(table[piece, :], xs[...])

    @pl.loop(0, half // 64)
    def _(i):
        upper, lower, first, weight = parts(i)
        xr, xi = xspec[upper, :], xspec[lower, :]
        hr, hi = tspec[upper, :], tspec[lower, :]
        hx = hi * xi
        prod_v[upper, :] = bf((hr * xr - jnp.where(first, 0.0, hx)) * weight)
        prod_v[lower, :] = bf(jnp.where(first, hx, hr * xi + hi * xr) * weight)

    @pl.loop(0, tokens // 256)
    def _(i):
        piece = pl.ds(pl.multiple_of(i * 256, 256), 256)
        back_v[piece, :] = bf(dot(turned[piece, :], prod_v[...]))

    v_moves = [
        send(2, step, peers[step], back_v.at[block(step), :], conv_in.at[:, own_cols])
        for step in steps
    ]
    conv_in[:, own_cols] = back_v[own_rows, :]

    for copy in c_moves:
        copy.wait_recv()

    @pl.loop(0, tokens // 256)
    def _(i):
        piece = pl.ds(pl.multiple_of(i * 256, 256), 256)
        cspec[piece, :] = dot(table[piece, :], cs[...])

    @pl.loop(0, half // 64)
    def _(i):
        upper, lower, first, weight = parts(i)
        xr, xi = xspec[upper, :], xspec[lower, :]
        cr, ci = cspec[upper, :], cspec[lower, :]
        hr, hi = tspec[upper, :], tspec[lower, :]
        cx, hc = ci * xi, hi * ci
        prod_t[upper, :] = bf((cr * xr + jnp.where(first, 0.0, cx)) * weight)
        prod_t[lower, :] = bf(jnp.where(first, cx, ci * xr - cr * xi) * weight)
        prod_g[upper, :] = bf((hr * cr + jnp.where(first, 0.0, hc)) * weight)
        prod_g[lower, :] = bf(jnp.where(first, hc, hr * ci - hi * cr) * weight)

    @pl.loop(0, window // 256)
    def _(i):
        piece = pl.ds(pl.multiple_of(i * 256, 256), 256)
        sums[piece, :] = dot(turned[piece, :], prod_t[...])

    folded = sums[0:period, :] * env[0:period, :]
    for at in range(1, window // period):
        piece = pl.ds(at * period, period)
        folded = folded + sums[piece, :] * env[piece, :]
    folded = bf(folded * (1.0 / math.sqrt(tokens * window)))
    gts[...] = folded
    gtall[:, own_cols] = folded
    first_hop = send(4, 0, across, gts, gtall.at[:, own_cols])
    near_hops = [send(4, step, near[step], gts, gtall.at[:, own_cols]) for step in near]

    @pl.loop(0, tokens // 256)
    def _(i):
        piece = pl.ds(pl.multiple_of(i * 256, 256), 256)
        back_g[piece, :] = bf(dot(turned[piece, :], prod_g[...]))

    g_moves = [
        send(3, step, peers[step], back_g.at[block(step), :], gi_ref.at[:, own_cols])
        for step in steps
    ]
    gi_ref[:, own_cols] = back_g[own_rows, :]

    first_hop.wait_recv()
    far_cols = pl.ds(pl.multiple_of(across * width, width), width)
    far_hops = [
        send(5, step, near[step], gtall.at[:, far_cols], gtall.at[:, far_cols]) for step in near
    ]
    for copy in near_hops + far_hops:
        copy.wait_recv()
    partial = dot(gtall[...], ow_hi[...], ((1,), (1,))) + dot(
        gtall[...], ow_lo[...], ((1,), (1,))
    )
    units[mine] = bf(partial)
    crossing = []
    for step in range(1, m):
        copy = pltpu.make_async_remote_copy(
            src_ref=units.at[mine], dst_ref=units.at[mine],
            send_sem=usend.at[step], recv_sem=urecv.at[step],
            device_id={"ch": others[step]}, device_id_type=MESH,
        )
        copy.start()
        crossing.append(copy)
    gow_ref[...] = dot(h_two_t, gtall[...])
    for copy in v_moves:
        copy.wait_recv()
    gg_ref[...] = bf(gout_ref[...].astype(jnp.float32) * conv_in[...].astype(jnp.float32))
    for copy in crossing:
        copy.wait()
    unit = units[0].astype(jnp.float32)
    for other in range(1, m):
        unit = unit + units[other].astype(jnp.float32)
    grad_two = unit * slope_two
    gw2_ref[...] = dot(h_one_t, grad_two, precision=full)
    gb2_ref[...] = jnp.sum(grad_two, axis=0, keepdims=True)
    grad_one = dot(grad_two, w2_ref[...], ((1,), (1,)), full) * slope_one
    gw1_ref[...] = dot(featt_ref[...], grad_one, precision=full)
    gb1_ref[...] = jnp.sum(grad_one, axis=0, keepdims=True)
    for copy in x_moves + c_moves + v_moves + near_hops + far_hops + [first_hop]:
        copy.wait_send()
    for copy in g_moves:
        copy.wait()


def drain_kernel(*refs):
    count = len(refs) // 2
    store_sem = refs[-1]
    stores = [
        pltpu.make_async_copy(refs[at], refs[count + at], store_sem.at[at])
        for at in range(count)
    ]
    for copy in stores:
        copy.start()
    for copy in stores:
        copy.wait()


def exchanged(
    mesh_shape, inputs, gate_values, grad_out, first_weight, first_bias, second_weight,
    second_bias, out_weight, decay_rates, mask_lengths,
):
    n, m = mesh_shape["seq"], mesh_shape["ch"]
    rows, channels = inputs.shape
    width = channels // n
    window = SPAN * rows
    emb, units = first_weight.shape
    period = 2 * emb
    tokens = n * rows
    angles = (
        2.0 * np.pi / period
        * (np.arange(period)[:, None] * (np.arange(emb // 2)[None, :] + 1) % period)
    )
    features = np.concatenate([np.cos(angles), np.sin(angles)], axis=1).astype(np.float32)
    f32, b16 = jnp.float32, jnp.bfloat16
    outside = pl.BlockSpec(memory_space=pltpu.HBM)
    inside = pl.BlockSpec(memory_space=pltpu.VMEM)
    shape = jax.ShapeDtypeStruct
    sem = pltpu.SemaphoreType.DMA
    table = packed_table(tokens)
    staged = (
        gate_values, grad_out, first_weight, first_bias[None], second_weight,
        second_bias[None], decay_rates[None], mask_lengths[None],
        jnp.asarray(features), jnp.asarray(features.T.copy()), out_weight,
        jnp.asarray(table, dtype=b16), jnp.asarray(table.T.copy(), dtype=b16),
    )
    out_shapes = (
        shape((rows, channels), b16), shape((rows, channels), b16),
        shape((emb, units), f32), shape((1, units), f32),
        shape((units, units), f32), shape((1, units), f32),
        shape((units, channels), f32),
    )
    outs = pl.pallas_call(
        functools.partial(exchange_kernel, (n, m, rows, width, window, period)),
        out_shape=tuple(pltpu.VMEM(out.shape, out.dtype) for out in out_shapes),
        in_specs=[outside] * 14,
        out_specs=(inside,) * 7,
        scratch_shapes=[
            *[pltpu.VMEM(array.shape, array.dtype) for array in staged],
            pltpu.VMEM((units, channels), b16), pltpu.VMEM((units, channels), b16),
            pltpu.VMEM((rows, channels), b16),
            pltpu.VMEM((tokens, width), b16), pltpu.VMEM((tokens, width), b16),
            pltpu.VMEM((rows, channels), b16),
            pltpu.VMEM((window, width), b16), pltpu.VMEM((window, width), f32),
            pltpu.VMEM((tokens, width), f32), pltpu.VMEM((tokens, width), f32),
            pltpu.VMEM((tokens, width), f32),
            pltpu.VMEM((tokens, width), b16), pltpu.VMEM((tokens, width), b16),
            pltpu.VMEM((tokens, width), b16),
            pltpu.VMEM((tokens, width), b16), pltpu.VMEM((tokens, width), b16),
            pltpu.VMEM((window, width), f32),
            pltpu.VMEM((period, width), b16), pltpu.VMEM((period, channels), b16),
            pltpu.VMEM((m, period, units), b16),
            sem((6, n)), sem((6, n)), sem((m,)), sem((m,)), sem((14,)),
        ],
        compiler_params=pltpu.CompilerParams(
            collective_id=0, has_side_effects=True, vmem_limit_bytes=VMEM_LIMIT
        ),
        name="exchange",
    )(*[pltpu.with_memory_space_constraint(array, pltpu.HBM) for array in (inputs, *staged)])
    outs = pl.pallas_call(
        drain_kernel,
        out_shape=out_shapes,
        in_specs=[inside] * 7,
        out_specs=(outside,) * 7,
        scratch_shapes=[sem((7,))],
        compiler_params=pltpu.CompilerParams(vmem_limit_bytes=DRAIN_LIMIT),
        name="drain",
    )(*outs)
    grad_in, gates, gw1, gb1, gw2, gb2, gow = outs
    return grad_in, gates, gw1, gb1[0], gw2, gb2[0], gow


def solution(mesh):
    def body(*arrays):
        rows, channels = arrays[0].shape
        count = mesh.shape["seq"]
        fits = channels == 128 * count and rows % 128 == 0 and count == 2 * SPAN
        if fits:
            return exchanged(mesh.shape, *arrays)
        return per_device(*arrays)

    in_specs = (
        P("seq", "ch"),
        P("seq", "ch"),
        P("seq", "ch"),
        P(),
        P(),
        P(),
        P(),
        P(None, "ch"),
        P("ch"),
        P("ch"),
    )
    out_specs = (P("seq", "ch"), P("seq", "ch"), P(), P(), P(), P(), P(None, "ch"))
    return jax.shard_map(
        body, mesh=mesh, in_specs=in_specs, out_specs=out_specs, check_vma=False
    )
```

```python
import math

import jax
import jax.numpy as jnp
import functools

import numpy as np
from jax import lax
from jax.experimental import pallas as pl
from jax.experimental.pallas import tpu as pltpu
from jax.sharding import PartitionSpec as P

SPAN = 4


FULL_PRECISION = lax.Precision.HIGHEST


def passed_along(value, axis, steps):
    count = lax.axis_size(axis)
    pairs = [(source, (source + steps) % count) for source in range(count)]
    return lax.ppermute(value, axis, pairs)


def angle_table(first_index, second_index, period):
    product = first_index[:, None] * second_index[None, :] % period
    return 2.0 * math.pi / period * product.astype(jnp.float32)


def lag_features(lag_count, feature_count):
    lag_index = jnp.arange(lag_count, dtype=jnp.int32)
    band_index = jnp.arange(feature_count // 2, dtype=jnp.int32) + 1
    phases = angle_table(lag_index, band_index, 2 * feature_count)
    return jnp.concatenate([jnp.cos(phases), jnp.sin(phases)], axis=1)


def split_table(table):
    upper_part = table.astype(jnp.bfloat16)
    lower_part = (table - upper_part.astype(jnp.float32)).astype(jnp.bfloat16)
    return (upper_part, lower_part)


def transform_tables(shard_rows):
    period = 2 * shard_rows
    frequency = jnp.arange(shard_rows + 1, dtype=jnp.int32)
    position = jnp.arange(shard_rows, dtype=jnp.int32)
    bin_weight = jnp.where((frequency == 0) | (frequency == shard_rows), 1.0, 2.0).astype(
        jnp.float32
    )
    forward_angles = angle_table(frequency, position, period)
    mirror_angles = angle_table(frequency, shard_rows - 1 - position, period)
    back_angles = angle_table(position + shard_rows, frequency, period)
    mirror_back = angle_table(2 * shard_rows - 1 - position, frequency, period)
    front_table = jnp.stack([jnp.cos(forward_angles), -jnp.sin(forward_angles)])
    mirror_table = jnp.stack([jnp.cos(mirror_angles), -jnp.sin(mirror_angles)])
    back_plain = jnp.stack([jnp.cos(back_angles), -jnp.sin(back_angles)]) / period
    back_table = back_plain * bin_weight[None, None, :]
    mirror_out = jnp.stack([jnp.cos(mirror_back), -jnp.sin(mirror_back)]) * (
        bin_weight[None, None, :] / period
    )
    fold_table = front_table * bin_weight[None, :, None]
    parity = (1.0 - 2.0 * (frequency % 2).astype(jnp.float32))[None, :, None]
    return (front_table, mirror_table, back_plain, back_table, mirror_out, fold_table, parity)


def spectrum(table_in, signal):
    return jnp.einsum("kfs,sc->kfc", table_in, signal, precision=FULL_PRECISION)


def sample_spectrum(table_pair, signal):
    upper_term = jnp.einsum(
        "kfs,sc->kfc", table_pair[0], signal, preferred_element_type=jnp.float32
    )
    lower_term = jnp.einsum(
        "kfs,sc->kfc", table_pair[1], signal, preferred_element_type=jnp.float32
    )
    return upper_term + lower_term


def sample_pullback(table_pair, signal):
    upper_term = jnp.einsum(
        "ksf,sc->kfc", table_pair[0], signal, preferred_element_type=jnp.float32
    )
    lower_term = jnp.einsum(
        "ksf,sc->kfc", table_pair[1], signal, preferred_element_type=jnp.float32
    )
    return upper_term + lower_term


def complex_product(left_factor, right_factor):
    real_part = left_factor[0] * right_factor[0] - left_factor[1] * right_factor[1]
    imag_part = left_factor[0] * right_factor[1] + left_factor[1] * right_factor[0]
    return jnp.stack([real_part, imag_part])


def conjugate_product(left_factor, right_factor):
    real_part = left_factor[0] * right_factor[0] + left_factor[1] * right_factor[1]
    imag_part = left_factor[1] * right_factor[0] - left_factor[0] * right_factor[1]
    return jnp.stack([real_part, imag_part])


def weighted_sum(filter_mixes, spectra_items):
    accumulated = complex_product(filter_mixes[0], spectra_items[0])
    for offset in range(1, len(filter_mixes)):
        accumulated = accumulated + complex_product(filter_mixes[offset], spectra_items[offset])
    return accumulated


def per_device(
    inputs,
    gate_values,
    grad_out,
    first_weight,
    first_bias,
    second_weight,
    second_bias,
    out_weight,
    decay_rates,
    mask_lengths,
):
    shard_rows = inputs.shape[0]
    window = SPAN * shard_rows
    front_table, mirror_table, back_plain, back_table, mirror_out, fold_table, parity = (
        transform_tables(shard_rows)
    )
    front_pair = split_table(front_table)
    mirror_pair = split_table(mirror_table)
    pull_pair = split_table(back_plain)
    features = lag_features(window, first_weight.shape[0])
    pre_first = jnp.dot(features, first_weight, precision=FULL_PRECISION) + first_bias
    hidden_one = jnp.sin(pre_first)
    pre_second = jnp.dot(hidden_one, second_weight, precision=FULL_PRECISION) + second_bias
    hidden_two = jnp.sin(pre_second)
    lag_index = jnp.arange(window, dtype=jnp.int32)
    envelope = jnp.exp(-decay_rates[None, :] * lag_index.astype(jnp.float32)[:, None]) * (
        lag_index[:, None] < mask_lengths[None, :]
    ).astype(jnp.float32)
    filter_taps = jnp.dot(hidden_two, out_weight, precision=FULL_PRECISION) * envelope
    block_spectra = [
        spectrum(front_table, filter_taps[block * shard_rows : (block + 1) * shard_rows])
        for block in range(SPAN)
    ]
    filter_mixes = []
    for offset in range(SPAN + 1):
        if offset == 0:
            mixed = parity * block_spectra[0]
        elif offset == SPAN:
            mixed = block_spectra[SPAN - 1]
        else:
            mixed = block_spectra[offset - 1] + parity * block_spectra[offset]
        filter_mixes.append(mixed)
    carried = (grad_out.astype(jnp.float32) * gate_values.astype(jnp.float32)).astype(jnp.bfloat16)
    earlier_spectra = [sample_spectrum(front_pair, inputs)]
    later_spectra = [sample_spectrum(mirror_pair, carried)]
    for offset in range(1, SPAN + 1):
        earlier = passed_along(inputs, "seq", offset)
        later = passed_along(carried, "seq", -offset)
        earlier_spectra.append(sample_spectrum(front_pair, earlier))
        later_spectra.append(sample_spectrum(mirror_pair, later))
    convolved = jnp.einsum(
        "ksf,kfc->sc",
        back_table,
        weighted_sum(filter_mixes, earlier_spectra),
        precision=FULL_PRECISION,
    )
    grad_gates = (grad_out.astype(jnp.float32) * convolved).astype(jnp.bfloat16)
    grad_inputs = jnp.einsum(
        "ksf,kfc->sc",
        mirror_out,
        weighted_sum(filter_mixes, later_spectra),
        precision=FULL_PRECISION,
    ).astype(jnp.bfloat16)
    pulled = sample_pullback(pull_pair, carried)
    grad_mixes = [conjugate_product(pulled, spectra_item) for spectra_item in earlier_spectra]
    pieces = []
    for block in range(SPAN):
        grad_block = parity * grad_mixes[block] + grad_mixes[block + 1]
        pieces.append(jnp.einsum("kfs,kfc->sc", fold_table, grad_block, precision=FULL_PRECISION))
    tap_terms = jnp.concatenate(pieces, axis=0)
    grad_scale = 1.0 / math.sqrt(lax.axis_size("seq") * shard_rows * window)
    tap_sums = lax.psum(tap_terms, "seq")
    grad_taps = tap_sums * envelope * grad_scale
    grad_out_weight = jnp.dot(hidden_two.T, grad_taps, precision=FULL_PRECISION)
    unit_grad = lax.psum(
        jnp.dot(grad_taps, out_weight.T, precision=FULL_PRECISION).astype(jnp.bfloat16), "ch"
    ).astype(jnp.float32)
    grad_two = unit_grad * jnp.cos(pre_second)
    grad_second_weight = jnp.dot(hidden_one.T, grad_two, precision=FULL_PRECISION)
    grad_second_bias = jnp.sum(grad_two, axis=0)
    grad_one = jnp.dot(grad_two, second_weight.T, precision=FULL_PRECISION) * jnp.cos(pre_first)
    grad_first_weight = jnp.dot(features.T, grad_one, precision=FULL_PRECISION)
    grad_first_bias = jnp.sum(grad_one, axis=0)
    return (
        grad_inputs,
        grad_gates,
        grad_first_weight,
        grad_first_bias,
        grad_second_weight,
        grad_second_bias,
        grad_out_weight,
    )


VMEM_LIMIT = 40_000_000
DRAIN_LIMIT = 8_000_000
EARLY, MIDDLE = 2, 4
MESH = pl.DeviceIdType.MESH


def bf(value):
    return value.astype(jnp.bfloat16)


def dot(left, right, dims=((1,), (0,)), precision=None):
    return lax.dot_general(
        left, right, (dims, ((), ())), precision=precision, preferred_element_type=jnp.float32
    )


def packed_table(tokens):
    half = tokens // 2
    freq = np.arange(half)[:, None]
    time = np.arange(tokens)[None, :]
    angles = 2.0 * np.pi / tokens * (freq * time % tokens)
    lower = -np.sin(angles)
    lower[0] = 1.0 - 2.0 * (np.arange(tokens) % 2)
    return np.concatenate([np.cos(angles), lower]).astype(np.float32)


def exchange_kernel(
    sizes, x_hbm, gate_hbm, gout_hbm, w1_hbm, b1_hbm, w2_hbm, b2_hbm, decay_hbm, mask_hbm,
    feat_hbm, featt_hbm, ow_hbm, table_hbm, turned_hbm,
    gi_ref, gg_ref, gw1_ref, gb1_ref, gw2_ref, gb2_ref, gow_ref,
    gate_ref, gout_ref, w1_ref, b1_ref, w2_ref, b2_ref, decay_ref, mask_ref,
    feat_ref, featt_ref, ow, table, turned,
    ow_hi, ow_lo, carried, xs, cs, conv_in, taps, env, xspec, cspec, tspec, prod_v, prod_t,
    prod_g, back_v, back_g, sums, gts, gtall, units, send_sem, recv_sem, usend, urecv,
    local_sem,
):
    n, m, rows, width, window, period = sizes
    tokens = n * rows
    half = tokens // 2
    me = lax.axis_index("seq")
    mine = lax.axis_index("ch")
    steps = range(1, n)
    peers = {step: lax.rem(me + step, n) for step in steps}
    others = {step: lax.rem(mine + step, m) for step in range(1, m)}

    barrier = pltpu.get_barrier_semaphore()
    for step in reversed(steps):
        pl.semaphore_signal(barrier, inc=1, device_id={"seq": peers[step]}, device_id_type=MESH)
    for step in range(1, m):
        pl.semaphore_signal(barrier, inc=1, device_id={"ch": others[step]}, device_id_type=MESH)

    own_rows = pl.ds(pl.multiple_of(me * rows, rows), rows)
    own_cols = pl.ds(pl.multiple_of(me * width, width), width)
    loads = []
    for at, (source, target) in enumerate((
        (gate_hbm, gate_ref), (gout_hbm, gout_ref), (x_hbm.at[:, own_cols], xs.at[own_rows, :]),
        (w1_hbm, w1_ref), (b1_hbm, b1_ref), (w2_hbm, w2_ref), (b2_hbm, b2_ref),
        (decay_hbm, decay_ref), (mask_hbm, mask_ref), (feat_hbm, feat_ref),
        (featt_hbm, featt_ref), (ow_hbm, ow), (table_hbm, table), (turned_hbm, turned),
    )):
        load = pltpu.make_async_copy(source, target, local_sem.at[at])
        load.start()
        loads.append(load)
    pl.semaphore_wait(barrier, n + m - 2)

    def send(kind, step, peer, source, target):
        copy = pltpu.make_async_remote_copy(
            src_ref=source, dst_ref=target,
            send_sem=send_sem.at[kind, step], recv_sem=recv_sem.at[kind, step],
            device_id={"seq": peer}, device_id_type=MESH,
        )
        copy.start()
        return copy

    def columns(step):
        return pl.ds(pl.multiple_of(peers[step] * width, width), width)

    def block(step):
        return pl.ds(pl.multiple_of(peers[step] * rows, rows), rows)

    x_moves = [
        send(0, step, peers[step], x_hbm.at[:, columns(step)], xs.at[own_rows, :])
        for step in steps
    ]
    for load in loads[:2]:
        load.wait()
    carried[...] = bf(gout_ref[...].astype(jnp.float32) * gate_ref[...].astype(jnp.float32))
    c_moves = [
        send(1, step, peers[step], carried.at[:, columns(step)], cs.at[own_rows, :])
        for step in steps
    ]
    cs[own_rows, :] = carried[:, own_cols]

    full = lax.Precision.HIGHEST
    for load in loads[2:]:
        load.wait()
    pre_one = dot(feat_ref[...], w1_ref[...], precision=full) + b1_ref[...]
    h_one = jnp.sin(pre_one)
    slope_one = jnp.cos(pre_one)
    pre_two = dot(h_one, w2_ref[...], precision=full) + b2_ref[...]
    h_two = jnp.sin(pre_two)
    slope_two = jnp.cos(pre_two)
    base = dot(h_two, ow[:, own_cols], precision=full)
    decay = decay_ref[:, own_cols]
    lengths = mask_ref[:, own_cols]
    for at in range(window // period):
        lag = lax.broadcasted_iota(jnp.int32, (period, width), 0) + at * period
        part = jnp.where(lag < lengths, jnp.exp(-decay * lag.astype(jnp.float32)), 0.0)
        env[pl.ds(at * period, period), :] = part
        taps[pl.ds(at * period, period), :] = bf(base * part)

    @pl.loop(0, tokens // 256)
    def _(i):
        piece = pl.ds(pl.multiple_of(i * 256, 256), 256)
        tspec[piece, :] = dot(table[piece, 0:window], taps[...])

    h_one_t = h_one.T
    upper_ow = bf(ow[...])
    ow_hi[...] = upper_ow
    ow_lo[...] = bf(ow[...] - upper_ow.astype(jnp.float32))
    h_two_t = bf(h_two.T)

    def parts(i):
        upper = pl.ds(pl.multiple_of(i * 64, 64), 64)
        lower = pl.ds(pl.multiple_of(half + i * 64, 64), 64)
        first = (lax.broadcasted_iota(jnp.int32, (64, width), 0) + i * 64) == 0
        weight = jnp.where(first, 1.0 / tokens, 2.0 / tokens)
        return upper, lower, first, weight

    for copy in x_moves:
        copy.wait_recv()

    @pl.loop(0, tokens // 256)
    def _(i):
        piece = pl.ds(pl.multiple_of(i * 256, 256), 256)
        xspec[piece, :] = dot(table[piece, :], xs[...])

    @pl.loop(0, half // 64)
    def _(i):
        upper, lower, first, weight = parts(i)
        xr, xi = xspec[upper, :], xspec[lower, :]
        hr, hi = tspec[upper, :], tspec[lower, :]
        hx = hi * xi
        prod_v[upper, :] = bf((hr * xr - jnp.where(first, 0.0, hx)) * weight)
        prod_v[lower, :] = bf(jnp.where(first, hx, hr * xi + hi * xr) * weight)

    @pl.loop(0, tokens // 256)
    def _(i):
        piece = pl.ds(pl.multiple_of(i * 256, 256), 256)
        back_v[piece, :] = bf(dot(turned[piece, :], prod_v[...]))

    v_moves = []

    def send_conv(some):
        for step in some:
            v_moves.append(
                send(2, step, peers[step], back_v.at[block(step), :], conv_in.at[:, own_cols])
            )

    send_conv(steps[:EARLY])
    conv_in[:, own_cols] = back_v[own_rows, :]

    for copy in c_moves:
        copy.wait_recv()

    @pl.loop(0, tokens // 256)
    def _(i):
        piece = pl.ds(pl.multiple_of(i * 256, 256), 256)
        cspec[piece, :] = dot(table[piece, :], cs[...])

    @pl.loop(0, half // 64)
    def _(i):
        upper, lower, first, weight = parts(i)
        xr, xi = xspec[upper, :], xspec[lower, :]
        cr, ci = cspec[upper, :], cspec[lower, :]
        cx = ci * xi
        prod_t[upper, :] = bf((cr * xr + jnp.where(first, 0.0, cx)) * weight)
        prod_t[lower, :] = bf(jnp.where(first, cx, ci * xr - cr * xi) * weight)

    @pl.loop(0, window // 256)
    def _(i):
        piece = pl.ds(pl.multiple_of(i * 256, 256), 256)
        sums[piece, :] = dot(turned[piece, :], prod_t[...])

    folded = sums[0:period, :] * env[0:period, :]
    for at in range(1, window // period):
        piece = pl.ds(at * period, period)
        folded = folded + sums[piece, :] * env[piece, :]
    folded = bf(folded * (1.0 / math.sqrt(tokens * window)))
    gts[...] = folded
    gtall[:, own_cols] = folded
    gathering = [
        send(4, step, peers[step], gts, gtall.at[:, own_cols])
        for step in sorted(steps, key=lambda step: -min(step, n - step))
    ]
    send_conv(steps[EARLY:MIDDLE])

    @pl.loop(0, half // 64)
    def _(i):
        upper, lower, first, weight = parts(i)
        cr, ci = cspec[upper, :], cspec[lower, :]
        hr, hi = tspec[upper, :], tspec[lower, :]
        hc = hi * ci
        prod_g[upper, :] = bf((hr * cr + jnp.where(first, 0.0, hc)) * weight)
        prod_g[lower, :] = bf(jnp.where(first, hc, hr * ci - hi * cr) * weight)

    @pl.loop(0, tokens // 256)
    def _(i):
        piece = pl.ds(pl.multiple_of(i * 256, 256), 256)
        back_g[piece, :] = bf(dot(turned[piece, :], prod_g[...]))

    send_conv(steps[MIDDLE:])
    g_moves = [
        send(3, step, peers[step], back_g.at[block(step), :], gi_ref.at[:, own_cols])
        for step in steps
    ]
    gi_ref[:, own_cols] = back_g[own_rows, :]
    for copy in gathering:
        copy.wait_recv()
    partial = dot(gtall[...], ow_hi[...], ((1,), (1,))) + dot(
        gtall[...], ow_lo[...], ((1,), (1,))
    )
    units[mine] = bf(partial)
    crossing = []
    for step in range(1, m):
        copy = pltpu.make_async_remote_copy(
            src_ref=units.at[mine], dst_ref=units.at[mine],
            send_sem=usend.at[step], recv_sem=urecv.at[step],
            device_id={"ch": others[step]}, device_id_type=MESH,
        )
        copy.start()
        crossing.append(copy)
    gow_ref[...] = dot(h_two_t, gtall[...])
    for copy in v_moves:
        copy.wait_recv()
    gg_ref[...] = bf(gout_ref[...].astype(jnp.float32) * conv_in[...].astype(jnp.float32))
    for copy in crossing:
        copy.wait()
    unit = units[0].astype(jnp.float32)
    for other in range(1, m):
        unit = unit + units[other].astype(jnp.float32)
    grad_two = unit * slope_two
    gw2_ref[...] = dot(h_one_t, grad_two, precision=full)
    gb2_ref[...] = jnp.sum(grad_two, axis=0, keepdims=True)
    grad_one = dot(grad_two, w2_ref[...], ((1,), (1,)), full) * slope_one
    gw1_ref[...] = dot(featt_ref[...], grad_one, precision=full)
    gb1_ref[...] = jnp.sum(grad_one, axis=0, keepdims=True)
    for copy in x_moves + c_moves + v_moves + gathering:
        copy.wait_send()
    for copy in g_moves:
        copy.wait()


def drain_kernel(*refs):
    count = len(refs) // 2
    store_sem = refs[-1]
    stores = [
        pltpu.make_async_copy(refs[at], refs[count + at], store_sem.at[at])
        for at in range(count)
    ]
    for copy in stores:
        copy.start()
    for copy in stores:
        copy.wait()


def exchanged(
    mesh_shape, inputs, gate_values, grad_out, first_weight, first_bias, second_weight,
    second_bias, out_weight, decay_rates, mask_lengths,
):
    n, m = mesh_shape["seq"], mesh_shape["ch"]
    rows, channels = inputs.shape
    width = channels // n
    window = SPAN * rows
    emb, units = first_weight.shape
    period = 2 * emb
    tokens = n * rows
    angles = (
        2.0 * np.pi / period
        * (np.arange(period)[:, None] * (np.arange(emb // 2)[None, :] + 1) % period)
    )
    features = np.concatenate([np.cos(angles), np.sin(angles)], axis=1).astype(np.float32)
    f32, b16 = jnp.float32, jnp.bfloat16
    outside = pl.BlockSpec(memory_space=pltpu.HBM)
    inside = pl.BlockSpec(memory_space=pltpu.VMEM)
    shape = jax.ShapeDtypeStruct
    sem = pltpu.SemaphoreType.DMA
    table = packed_table(tokens)
    staged = (
        gate_values, grad_out, first_weight, first_bias[None], second_weight,
        second_bias[None], decay_rates[None], mask_lengths[None],
        jnp.asarray(features), jnp.asarray(features.T.copy()), out_weight,
        jnp.asarray(table, dtype=b16), jnp.asarray(table.T.copy(), dtype=b16),
    )
    out_shapes = (
        shape((rows, channels), b16), shape((rows, channels), b16),
        shape((emb, units), f32), shape((1, units), f32),
        shape((units, units), f32), shape((1, units), f32),
        shape((units, channels), f32),
    )
    outs = pl.pallas_call(
        functools.partial(exchange_kernel, (n, m, rows, width, window, period)),
        out_shape=tuple(pltpu.VMEM(out.shape, out.dtype) for out in out_shapes),
        in_specs=[outside] * 14,
        out_specs=(inside,) * 7,
        scratch_shapes=[
            *[pltpu.VMEM(array.shape, array.dtype) for array in staged],
            pltpu.VMEM((units, channels), b16), pltpu.VMEM((units, channels), b16),
            pltpu.VMEM((rows, channels), b16),
            pltpu.VMEM((tokens, width), b16), pltpu.VMEM((tokens, width), b16),
            pltpu.VMEM((rows, channels), b16),
            pltpu.VMEM((window, width), b16), pltpu.VMEM((window, width), f32),
            pltpu.VMEM((tokens, width), f32), pltpu.VMEM((tokens, width), f32),
            pltpu.VMEM((tokens, width), f32),
            pltpu.VMEM((tokens, width), b16), pltpu.VMEM((tokens, width), b16),
            pltpu.VMEM((tokens, width), b16),
            pltpu.VMEM((tokens, width), b16), pltpu.VMEM((tokens, width), b16),
            pltpu.VMEM((window, width), f32),
            pltpu.VMEM((period, width), b16), pltpu.VMEM((period, channels), b16),
            pltpu.VMEM((m, period, units), b16),
            sem((6, n)), sem((6, n)), sem((m,)), sem((m,)), sem((14,)),
        ],
        compiler_params=pltpu.CompilerParams(
            collective_id=0, has_side_effects=True, vmem_limit_bytes=VMEM_LIMIT
        ),
        name="exchange",
    )(*[pltpu.with_memory_space_constraint(array, pltpu.HBM) for array in (inputs, *staged)])
    outs = pl.pallas_call(
        drain_kernel,
        out_shape=out_shapes,
        in_specs=[inside] * 7,
        out_specs=(outside,) * 7,
        scratch_shapes=[sem((7,))],
        compiler_params=pltpu.CompilerParams(vmem_limit_bytes=DRAIN_LIMIT),
        name="drain",
    )(*outs)
    grad_in, gates, gw1, gb1, gw2, gb2, gow = outs
    return grad_in, gates, gw1, gb1[0], gw2, gb2[0], gow


def solution(mesh):
    def body(*arrays):
        rows, channels = arrays[0].shape
        count = mesh.shape["seq"]
        fits = channels == 128 * count and rows % 128 == 0 and count == 2 * SPAN
        if fits:
            return exchanged(mesh.shape, *arrays)
        return per_device(*arrays)

    in_specs = (
        P("seq", "ch"),
        P("seq", "ch"),
        P("seq", "ch"),
        P(),
        P(),
        P(),
        P(),
        P(None, "ch"),
        P("ch"),
        P("ch"),
    )
    out_specs = (P("seq", "ch"), P("seq", "ch"), P(), P(), P(), P(), P(None, "ch"))
    return jax.shard_map(
        body, mesh=mesh, in_specs=in_specs, out_specs=out_specs, check_vma=False
    )
```

```python
import math

import jax
import jax.numpy as jnp
import functools

import numpy as np
from jax import lax
from jax.experimental import pallas as pl
from jax.experimental.pallas import tpu as pltpu
from jax.sharding import PartitionSpec as P

SPAN = 4


FULL_PRECISION = lax.Precision.HIGHEST


def passed_along(value, axis, steps):
    count = lax.axis_size(axis)
    pairs = [(source, (source + steps) % count) for source in range(count)]
    return lax.ppermute(value, axis, pairs)


def angle_table(first_index, second_index, period):
    product = first_index[:, None] * second_index[None, :] % period
    return 2.0 * math.pi / period * product.astype(jnp.float32)


def lag_features(lag_count, feature_count):
    lag_index = jnp.arange(lag_count, dtype=jnp.int32)
    band_index = jnp.arange(feature_count // 2, dtype=jnp.int32) + 1
    phases = angle_table(lag_index, band_index, 2 * feature_count)
    return jnp.concatenate([jnp.cos(phases), jnp.sin(phases)], axis=1)


def split_table(table):
    upper_part = table.astype(jnp.bfloat16)
    lower_part = (table - upper_part.astype(jnp.float32)).astype(jnp.bfloat16)
    return (upper_part, lower_part)


def transform_tables(shard_rows):
    period = 2 * shard_rows
    frequency = jnp.arange(shard_rows + 1, dtype=jnp.int32)
    position = jnp.arange(shard_rows, dtype=jnp.int32)
    bin_weight = jnp.where((frequency == 0) | (frequency == shard_rows), 1.0, 2.0).astype(
        jnp.float32
    )
    forward_angles = angle_table(frequency, position, period)
    mirror_angles = angle_table(frequency, shard_rows - 1 - position, period)
    back_angles = angle_table(position + shard_rows, frequency, period)
    mirror_back = angle_table(2 * shard_rows - 1 - position, frequency, period)
    front_table = jnp.stack([jnp.cos(forward_angles), -jnp.sin(forward_angles)])
    mirror_table = jnp.stack([jnp.cos(mirror_angles), -jnp.sin(mirror_angles)])
    back_plain = jnp.stack([jnp.cos(back_angles), -jnp.sin(back_angles)]) / period
    back_table = back_plain * bin_weight[None, None, :]
    mirror_out = jnp.stack([jnp.cos(mirror_back), -jnp.sin(mirror_back)]) * (
        bin_weight[None, None, :] / period
    )
    fold_table = front_table * bin_weight[None, :, None]
    parity = (1.0 - 2.0 * (frequency % 2).astype(jnp.float32))[None, :, None]
    return (front_table, mirror_table, back_plain, back_table, mirror_out, fold_table, parity)


def spectrum(table_in, signal):
    return jnp.einsum("kfs,sc->kfc", table_in, signal, precision=FULL_PRECISION)


def sample_spectrum(table_pair, signal):
    upper_term = jnp.einsum(
        "kfs,sc->kfc", table_pair[0], signal, preferred_element_type=jnp.float32
    )
    lower_term = jnp.einsum(
        "kfs,sc->kfc", table_pair[1], signal, preferred_element_type=jnp.float32
    )
    return upper_term + lower_term


def sample_pullback(table_pair, signal):
    upper_term = jnp.einsum(
        "ksf,sc->kfc", table_pair[0], signal, preferred_element_type=jnp.float32
    )
    lower_term = jnp.einsum(
        "ksf,sc->kfc", table_pair[1], signal, preferred_element_type=jnp.float32
    )
    return upper_term + lower_term


def complex_product(left_factor, right_factor):
    real_part = left_factor[0] * right_factor[0] - left_factor[1] * right_factor[1]
    imag_part = left_factor[0] * right_factor[1] + left_factor[1] * right_factor[0]
    return jnp.stack([real_part, imag_part])


def conjugate_product(left_factor, right_factor):
    real_part = left_factor[0] * right_factor[0] + left_factor[1] * right_factor[1]
    imag_part = left_factor[1] * right_factor[0] - left_factor[0] * right_factor[1]
    return jnp.stack([real_part, imag_part])


def weighted_sum(filter_mixes, spectra_items):
    accumulated = complex_product(filter_mixes[0], spectra_items[0])
    for offset in range(1, len(filter_mixes)):
        accumulated = accumulated + complex_product(filter_mixes[offset], spectra_items[offset])
    return accumulated


def per_device(
    inputs,
    gate_values,
    grad_out,
    first_weight,
    first_bias,
    second_weight,
    second_bias,
    out_weight,
    decay_rates,
    mask_lengths,
):
    shard_rows = inputs.shape[0]
    window = SPAN * shard_rows
    front_table, mirror_table, back_plain, back_table, mirror_out, fold_table, parity = (
        transform_tables(shard_rows)
    )
    front_pair = split_table(front_table)
    mirror_pair = split_table(mirror_table)
    pull_pair = split_table(back_plain)
    features = lag_features(window, first_weight.shape[0])
    pre_first = jnp.dot(features, first_weight, precision=FULL_PRECISION) + first_bias
    hidden_one = jnp.sin(pre_first)
    pre_second = jnp.dot(hidden_one, second_weight, precision=FULL_PRECISION) + second_bias
    hidden_two = jnp.sin(pre_second)
    lag_index = jnp.arange(window, dtype=jnp.int32)
    envelope = jnp.exp(-decay_rates[None, :] * lag_index.astype(jnp.float32)[:, None]) * (
        lag_index[:, None] < mask_lengths[None, :]
    ).astype(jnp.float32)
    filter_taps = jnp.dot(hidden_two, out_weight, precision=FULL_PRECISION) * envelope
    block_spectra = [
        spectrum(front_table, filter_taps[block * shard_rows : (block + 1) * shard_rows])
        for block in range(SPAN)
    ]
    filter_mixes = []
    for offset in range(SPAN + 1):
        if offset == 0:
            mixed = parity * block_spectra[0]
        elif offset == SPAN:
            mixed = block_spectra[SPAN - 1]
        else:
            mixed = block_spectra[offset - 1] + parity * block_spectra[offset]
        filter_mixes.append(mixed)
    carried = (grad_out.astype(jnp.float32) * gate_values.astype(jnp.float32)).astype(jnp.bfloat16)
    earlier_spectra = [sample_spectrum(front_pair, inputs)]
    later_spectra = [sample_spectrum(mirror_pair, carried)]
    for offset in range(1, SPAN + 1):
        earlier = passed_along(inputs, "seq", offset)
        later = passed_along(carried, "seq", -offset)
        earlier_spectra.append(sample_spectrum(front_pair, earlier))
        later_spectra.append(sample_spectrum(mirror_pair, later))
    convolved = jnp.einsum(
        "ksf,kfc->sc",
        back_table,
        weighted_sum(filter_mixes, earlier_spectra),
        precision=FULL_PRECISION,
    )
    grad_gates = (grad_out.astype(jnp.float32) * convolved).astype(jnp.bfloat16)
    grad_inputs = jnp.einsum(
        "ksf,kfc->sc",
        mirror_out,
        weighted_sum(filter_mixes, later_spectra),
        precision=FULL_PRECISION,
    ).astype(jnp.bfloat16)
    pulled = sample_pullback(pull_pair, carried)
    grad_mixes = [conjugate_product(pulled, spectra_item) for spectra_item in earlier_spectra]
    pieces = []
    for block in range(SPAN):
        grad_block = parity * grad_mixes[block] + grad_mixes[block + 1]
        pieces.append(jnp.einsum("kfs,kfc->sc", fold_table, grad_block, precision=FULL_PRECISION))
    tap_terms = jnp.concatenate(pieces, axis=0)
    grad_scale = 1.0 / math.sqrt(lax.axis_size("seq") * shard_rows * window)
    tap_sums = lax.psum(tap_terms, "seq")
    grad_taps = tap_sums * envelope * grad_scale
    grad_out_weight = jnp.dot(hidden_two.T, grad_taps, precision=FULL_PRECISION)
    unit_grad = lax.psum(
        jnp.dot(grad_taps, out_weight.T, precision=FULL_PRECISION).astype(jnp.bfloat16), "ch"
    ).astype(jnp.float32)
    grad_two = unit_grad * jnp.cos(pre_second)
    grad_second_weight = jnp.dot(hidden_one.T, grad_two, precision=FULL_PRECISION)
    grad_second_bias = jnp.sum(grad_two, axis=0)
    grad_one = jnp.dot(grad_two, second_weight.T, precision=FULL_PRECISION) * jnp.cos(pre_first)
    grad_first_weight = jnp.dot(features.T, grad_one, precision=FULL_PRECISION)
    grad_first_bias = jnp.sum(grad_one, axis=0)
    return (
        grad_inputs,
        grad_gates,
        grad_first_weight,
        grad_first_bias,
        grad_second_weight,
        grad_second_bias,
        grad_out_weight,
    )


VMEM_LIMIT = 40_000_000
DRAIN_LIMIT = 8_000_000
EARLY, MIDDLE = 3, 5
MESH = pl.DeviceIdType.MESH


def bf(value):
    return value.astype(jnp.bfloat16)


def dot(left, right, dims=((1,), (0,)), precision=None):
    return lax.dot_general(
        left, right, (dims, ((), ())), precision=precision, preferred_element_type=jnp.float32
    )


def packed_table(tokens):
    half = tokens // 2
    freq = np.arange(half)[:, None]
    time = np.arange(tokens)[None, :]
    angles = 2.0 * np.pi / tokens * (freq * time % tokens)
    lower = -np.sin(angles)
    lower[0] = 1.0 - 2.0 * (np.arange(tokens) % 2)
    return np.concatenate([np.cos(angles), lower]).astype(np.float32)


def exchange_kernel(
    sizes, x_hbm, gate_hbm, gout_hbm, w1_hbm, b1_hbm, w2_hbm, b2_hbm, decay_hbm, mask_hbm,
    feat_hbm, featt_hbm, ow_hbm, table_hbm, turned_hbm,
    gi_ref, gg_ref, gw1_ref, gb1_ref, gw2_ref, gb2_ref, gow_ref,
    gate_ref, gout_ref, w1_ref, b1_ref, w2_ref, b2_ref, decay_ref, mask_ref,
    feat_ref, featt_ref, ow, table, turned,
    ow_turned, carried, xs, cs, conv_in, taps, env, xspec, cspec, tspec, prod_v, prod_t,
    prod_g, back_v, back_g, sums, gts, gtall, units, send_sem, recv_sem, usend, urecv,
    local_sem, late_sem,
):
    n, m, rows, width, window, period = sizes
    tokens = n * rows
    half = tokens // 2
    side = n // 2
    me = lax.axis_index("seq")
    mine = lax.axis_index("ch")
    late = n - n // 4
    steps = range(1, n)
    others = {step: lax.rem(mine + step, m) for step in range(1, m)}
    upper_side = me >= side
    lower_side = me < side
    base_peer = me // side * side
    near = [base_peer + lax.rem(me - base_peer + step, side) for step in range(1, side)]
    across = lax.rem(me + side, n)
    far = [side - base_peer + lax.rem(me - base_peer + step, side) for step in range(side)]

    barrier = pltpu.get_barrier_semaphore()

    def greet(peer):
        pl.semaphore_signal(barrier, inc=1, device_id={"seq": peer}, device_id_type=MESH)

    @pl.when(me < late)
    def _():
        for peer in far:
            greet(peer)

    for peer in near:
        greet(peer)
    for step in range(1, m):
        pl.semaphore_signal(barrier, inc=1, device_id={"ch": others[step]}, device_id_type=MESH)

    own_rows = pl.ds(pl.multiple_of(me * rows, rows), rows)
    own_cols = pl.ds(pl.multiple_of(me * width, width), width)
    loads = []
    for at, (source, target) in enumerate((
        (gate_hbm, gate_ref), (gout_hbm, gout_ref), (x_hbm.at[:, own_cols], xs.at[own_rows, :]),
        (w1_hbm, w1_ref), (b1_hbm, b1_ref), (w2_hbm, w2_ref), (b2_hbm, b2_ref),
        (decay_hbm, decay_ref), (mask_hbm, mask_ref), (feat_hbm, feat_ref),
        (featt_hbm, featt_ref), (ow_hbm, ow), (table_hbm, table), (turned_hbm, turned),
    )):
        load = pltpu.make_async_copy(source, target, local_sem.at[at])
        load.start()
        loads.append(load)
    missing = jnp.where(lower_side, n - late, 0)
    pl.semaphore_wait(barrier, n + m - 2 - missing)

    @pl.when((me >= side) & (me < late))
    def _():
        for at in range(side // (late - side)):
            pl.semaphore_signal(
                late_sem, inc=1, device_id_type=MESH,
                device_id={"seq": (me - side) * (side // (late - side)) + at},
            )

    def move(kind, step, source, target):
        return pltpu.make_async_remote_copy(
            src_ref=source, dst_ref=target,
            send_sem=send_sem.at[kind, step], recv_sem=recv_sem.at[kind, step],
            device_id={"seq": lax.rem(me + step, n)}, device_id_type=MESH,
        )

    def ahead(peer):
        return lax.rem(peer - me + n, n)

    def columns(peer):
        return pl.ds(pl.multiple_of(peer * width, width), width)

    def block(peer):
        return pl.ds(pl.multiple_of(peer * rows, rows), rows)

    x_moves = [move(0, step, xs.at[own_rows, :], xs.at[own_rows, :]) for step in steps]
    c_moves = [move(1, step, cs.at[own_rows, :], cs.at[own_rows, :]) for step in steps]
    for at in range(n - 1):
        around = lax.rem(me + 1 + at, n)
        early = lax.rem(me + 1 + at, late) if at < late - 1 else at + 1
        peer = jnp.where(lower_side, early, around)
        if at == late - 1:

            @pl.when(lower_side)
            def _():
                pl.semaphore_wait(late_sem, 1)

        move(0, ahead(peer), x_hbm.at[:, columns(peer)], xs.at[own_rows, :]).start()
    for load in loads[:2]:
        load.wait()
    carried[...] = bf(gout_ref[...].astype(jnp.float32) * gate_ref[...].astype(jnp.float32))
    for step in steps:
        peer = lax.rem(me + step, n)
        move(1, step, carried.at[:, columns(peer)], cs.at[own_rows, :]).start()
    cs[own_rows, :] = carried[:, own_cols]

    full = lax.Precision.HIGHEST
    for load in loads[2:]:
        load.wait()
    pre_one = dot(feat_ref[...], w1_ref[...], precision=full) + b1_ref[...]
    h_one = jnp.sin(pre_one)
    slope_one = jnp.cos(pre_one)
    pre_two = dot(h_one, w2_ref[...], precision=full) + b2_ref[...]
    h_two = jnp.sin(pre_two)
    slope_two = jnp.cos(pre_two)
    base = dot(h_two, ow[:, own_cols], precision=full)
    decay = decay_ref[:, own_cols]
    lengths = mask_ref[:, own_cols]
    for at in range(window // period):
        lag = lax.broadcasted_iota(jnp.int32, (period, width), 0) + at * period
        part = jnp.where(lag < lengths, jnp.exp(-decay * lag.astype(jnp.float32)), 0.0)
        env[pl.ds(at * period, period), :] = part
        taps[pl.ds(at * period, period), :] = bf(base * part)

    tspec[...] = dot(table[:, 0:window], taps[...])

    h_one_t = bf(h_one.T)
    w2_turned = bf(w2_ref[...].T)
    featt = bf(featt_ref[...])
    ow_turned[...] = bf(ow[...].T)
    h_two_t = bf(h_two.T)

    def parts(i):
        upper = pl.ds(pl.multiple_of(i * 64, 64), 64)
        lower = pl.ds(pl.multiple_of(half + i * 64, 64), 64)
        first = (lax.broadcasted_iota(jnp.int32, (64, width), 0) + i * 64) == 0
        weight = jnp.where(first, 1.0 / tokens, 2.0 / tokens)
        return upper, lower, first, weight

    for copy in x_moves:
        copy.wait_recv()

    xspec[...] = dot(table[...], xs[...])

    @pl.loop(0, half // 64)
    def _(i):
        upper, lower, first, weight = parts(i)
        xr, xi = xspec[upper, :], xspec[lower, :]
        hr, hi = tspec[upper, :], tspec[lower, :]
        hx = hi * xi
        prod_v[upper, :] = bf((hr * xr - jnp.where(first, 0.0, hx)) * weight)
        prod_v[lower, :] = bf(jnp.where(first, hx, hr * xi + hi * xr) * weight)

    back_v[...] = bf(dot(turned[...], prod_v[...]))

    v_moves = [
        move(2, step, back_v.at[own_rows, :], conv_in.at[:, own_cols]) for step in steps
    ]

    def send_conv(some):
        for step in some:
            peer = lax.rem(me + step, n)
            move(2, step, back_v.at[block(peer), :], conv_in.at[:, own_cols]).start()

    send_conv(steps[:EARLY])
    conv_in[:, own_cols] = back_v[own_rows, :]

    for copy in c_moves:
        copy.wait_recv()

    cspec[...] = dot(table[...], cs[...])

    @pl.loop(0, half // 64)
    def _(i):
        upper, lower, first, weight = parts(i)
        xr, xi = xspec[upper, :], xspec[lower, :]
        cr, ci = cspec[upper, :], cspec[lower, :]
        cx = ci * xi
        prod_t[upper, :] = bf((cr * xr + jnp.where(first, 0.0, cx)) * weight)
        prod_t[lower, :] = bf(jnp.where(first, cx, ci * xr - cr * xi) * weight)

    sums[...] = dot(turned[0:window, :], prod_t[...])

    folded = sums[0:period, :] * env[0:period, :]
    for at in range(1, window // period):
        piece = pl.ds(at * period, period)
        folded = folded + sums[piece, :] * env[piece, :]
    folded = bf(folded * (1.0 / math.sqrt(tokens * window)))
    gts[...] = folded
    gtall[:, own_cols] = folded

    def give(peer):
        return move(4, ahead(peer), gts, gtall.at[:, own_cols])

    def taken(kind, peer):
        return move(kind, lax.rem(me - peer + n, n), gts, gtall.at[:, own_cols])

    give(across).start()

    for peer in near:
        give(peer).start()
    send_conv(steps[EARLY:MIDDLE])

    @pl.loop(0, half // 64)
    def _(i):
        upper, lower, first, weight = parts(i)
        cr, ci = cspec[upper, :], cspec[lower, :]
        hr, hi = tspec[upper, :], tspec[lower, :]
        hc = hi * ci
        prod_g[upper, :] = bf((hr * cr + jnp.where(first, 0.0, hc)) * weight)
        prod_g[lower, :] = bf(jnp.where(first, hc, hr * ci - hi * cr) * weight)

    back_g[...] = bf(dot(turned[...], prod_g[...]))


    def forward(peer):
        return move(5, ahead(peer), gtall.at[:, columns(across)], gtall.at[:, columns(across)])

    taken(4, across).wait_recv()
    for peer in near:
        forward(peer).start()

    send_conv(steps[MIDDLE:])
    g_moves = [move(3, step, back_g.at[own_rows, :], gi_ref.at[:, own_cols]) for step in steps]
    for step in steps:
        peer = lax.rem(me + step, n)
        move(3, step, back_g.at[block(peer), :], gi_ref.at[:, own_cols]).start()
    gi_ref[:, own_cols] = back_g[own_rows, :]
    for peer in near:
        taken(4, peer).wait_recv()

    for peer in near:
        taken(5, peer).wait_recv()

    units[mine] = bf(dot(gtall[...], ow_turned[...]))
    crossing = []
    for step in range(1, m):
        copy = pltpu.make_async_remote_copy(
            src_ref=units.at[mine], dst_ref=units.at[mine],
            send_sem=usend.at[step], recv_sem=urecv.at[step],
            device_id={"ch": others[step]}, device_id_type=MESH,
        )
        copy.start()
        crossing.append(copy)
    gow_ref[...] = dot(h_two_t, gtall[...])
    for copy in v_moves:
        copy.wait_recv()
    gg_ref[...] = bf(gout_ref[...].astype(jnp.float32) * conv_in[...].astype(jnp.float32))
    for copy in crossing:
        copy.wait_recv()
    unit = units[0].astype(jnp.float32)
    for other in range(1, m):
        unit = unit + units[other].astype(jnp.float32)
    grad_two = unit * slope_two
    narrow_two = bf(grad_two)
    grad_one = dot(narrow_two, w2_turned) * slope_one
    gw1_ref[...] = dot(featt, bf(grad_one))
    gw2_ref[...] = dot(h_one_t, narrow_two)
    gb2_ref[...] = jnp.sum(grad_two, axis=0, keepdims=True)
    gb1_ref[...] = jnp.sum(grad_one, axis=0, keepdims=True)
    for copy in x_moves + c_moves + v_moves:
        copy.wait_send()
    for peer in near:
        give(peer).wait_send()

    give(across).wait_send()
    for peer in near:
        forward(peer).wait_send()
    for copy in crossing:
        copy.wait_send()
    for copy in g_moves:
        copy.wait()


def drain_kernel(*refs):
    count = len(refs) // 2
    store_sem = refs[-1]
    stores = [
        pltpu.make_async_copy(refs[at], refs[count + at], store_sem.at[at])
        for at in range(count)
    ]
    for copy in stores:
        copy.start()
    for copy in stores:
        copy.wait()


def exchanged(
    mesh_shape, inputs, gate_values, grad_out, first_weight, first_bias, second_weight,
    second_bias, out_weight, decay_rates, mask_lengths,
):
    n, m = mesh_shape["seq"], mesh_shape["ch"]
    rows, channels = inputs.shape
    width = channels // n
    window = SPAN * rows
    emb, units = first_weight.shape
    period = 2 * emb
    tokens = n * rows
    angles = (
        2.0 * np.pi / period
        * (np.arange(period)[:, None] * (np.arange(emb // 2)[None, :] + 1) % period)
    )
    features = np.concatenate([np.cos(angles), np.sin(angles)], axis=1).astype(np.float32)
    f32, b16 = jnp.float32, jnp.bfloat16
    outside = pl.BlockSpec(memory_space=pltpu.HBM)
    inside = pl.BlockSpec(memory_space=pltpu.VMEM)
    shape = jax.ShapeDtypeStruct
    sem = pltpu.SemaphoreType.DMA
    table = packed_table(tokens)
    staged = (
        gate_values, grad_out, first_weight, first_bias[None], second_weight,
        second_bias[None], decay_rates[None], mask_lengths[None],
        jnp.asarray(features), jnp.asarray(features.T.copy()), out_weight,
        jnp.asarray(table, dtype=b16), jnp.asarray(table.T.copy(), dtype=b16),
    )
    out_shapes = (
        shape((rows, channels), b16), shape((rows, channels), b16),
        shape((emb, units), f32), shape((1, units), f32),
        shape((units, units), f32), shape((1, units), f32),
        shape((units, channels), f32),
    )
    outs = pl.pallas_call(
        functools.partial(exchange_kernel, (n, m, rows, width, window, period)),
        out_shape=tuple(pltpu.VMEM(out.shape, out.dtype) for out in out_shapes),
        in_specs=[outside] * 14,
        out_specs=(inside,) * 7,
        scratch_shapes=[
            *[pltpu.VMEM(array.shape, array.dtype) for array in staged],
            pltpu.VMEM((channels, units), b16),
            pltpu.VMEM((rows, channels), b16),
            pltpu.VMEM((tokens, width), b16), pltpu.VMEM((tokens, width), b16),
            pltpu.VMEM((rows, channels), b16),
            pltpu.VMEM((window, width), b16), pltpu.VMEM((window, width), f32),
            pltpu.VMEM((tokens, width), f32), pltpu.VMEM((tokens, width), f32),
            pltpu.VMEM((tokens, width), f32),
            pltpu.VMEM((tokens, width), b16), pltpu.VMEM((tokens, width), b16),
            pltpu.VMEM((tokens, width), b16),
            pltpu.VMEM((tokens, width), b16), pltpu.VMEM((tokens, width), b16),
            pltpu.VMEM((window, width), f32),
            pltpu.VMEM((period, width), b16), pltpu.VMEM((period, channels), b16),
            pltpu.VMEM((m, period, units), b16),
            sem((6, n)), sem((6, n)), sem((m,)), sem((m,)), sem((14,)),
            pltpu.SemaphoreType.REGULAR,
        ],
        compiler_params=pltpu.CompilerParams(
            collective_id=0, has_side_effects=True, vmem_limit_bytes=VMEM_LIMIT
        ),
        name="exchange",
    )(*[pltpu.with_memory_space_constraint(array, pltpu.HBM) for array in (inputs, *staged)])
    outs = pl.pallas_call(
        drain_kernel,
        out_shape=out_shapes,
        in_specs=[inside] * 7,
        out_specs=(outside,) * 7,
        scratch_shapes=[sem((7,))],
        compiler_params=pltpu.CompilerParams(vmem_limit_bytes=DRAIN_LIMIT),
        name="drain",
    )(*outs)
    grad_in, gates, gw1, gb1, gw2, gb2, gow = outs
    return grad_in, gates, gw1, gb1[0], gw2, gb2[0], gow


def solution(mesh):
    def body(*arrays):
        rows, channels = arrays[0].shape
        count = mesh.shape["seq"]
        fits = channels == 128 * count and rows % 128 == 0 and count == 2 * SPAN
        if fits:
            return exchanged(mesh.shape, *arrays)
        return per_device(*arrays)

    in_specs = (
        P("seq", "ch"),
        P("seq", "ch"),
        P("seq", "ch"),
        P(),
        P(),
        P(),
        P(),
        P(None, "ch"),
        P("ch"),
        P("ch"),
    )
    out_specs = (P("seq", "ch"), P("seq", "ch"), P(), P(), P(), P(), P(None, "ch"))
    return jax.shard_map(
        body, mesh=mesh, in_specs=in_specs, out_specs=out_specs, check_vma=False
    )
```

```python
import math

import jax
import jax.numpy as jnp
import functools

import numpy as np
from jax import lax
from jax.experimental import pallas as pl
from jax.experimental.pallas import tpu as pltpu
from jax.sharding import PartitionSpec as P

SPAN = 4


FULL_PRECISION = lax.Precision.HIGHEST


def passed_along(value, axis, steps):
    count = lax.axis_size(axis)
    pairs = [(source, (source + steps) % count) for source in range(count)]
    return lax.ppermute(value, axis, pairs)


def angle_table(first_index, second_index, period):
    product = first_index[:, None] * second_index[None, :] % period
    return 2.0 * math.pi / period * product.astype(jnp.float32)


def lag_features(lag_count, feature_count):
    lag_index = jnp.arange(lag_count, dtype=jnp.int32)
    band_index = jnp.arange(feature_count // 2, dtype=jnp.int32) + 1
    phases = angle_table(lag_index, band_index, 2 * feature_count)
    return jnp.concatenate([jnp.cos(phases), jnp.sin(phases)], axis=1)


def split_table(table):
    upper_part = table.astype(jnp.bfloat16)
    lower_part = (table - upper_part.astype(jnp.float32)).astype(jnp.bfloat16)
    return (upper_part, lower_part)


def transform_tables(shard_rows):
    period = 2 * shard_rows
    frequency = jnp.arange(shard_rows + 1, dtype=jnp.int32)
    position = jnp.arange(shard_rows, dtype=jnp.int32)
    bin_weight = jnp.where((frequency == 0) | (frequency == shard_rows), 1.0, 2.0).astype(
        jnp.float32
    )
    forward_angles = angle_table(frequency, position, period)
    mirror_angles = angle_table(frequency, shard_rows - 1 - position, period)
    back_angles = angle_table(position + shard_rows, frequency, period)
    mirror_back = angle_table(2 * shard_rows - 1 - position, frequency, period)
    front_table = jnp.stack([jnp.cos(forward_angles), -jnp.sin(forward_angles)])
    mirror_table = jnp.stack([jnp.cos(mirror_angles), -jnp.sin(mirror_angles)])
    back_plain = jnp.stack([jnp.cos(back_angles), -jnp.sin(back_angles)]) / period
    back_table = back_plain * bin_weight[None, None, :]
    mirror_out = jnp.stack([jnp.cos(mirror_back), -jnp.sin(mirror_back)]) * (
        bin_weight[None, None, :] / period
    )
    fold_table = front_table * bin_weight[None, :, None]
    parity = (1.0 - 2.0 * (frequency % 2).astype(jnp.float32))[None, :, None]
    return (front_table, mirror_table, back_plain, back_table, mirror_out, fold_table, parity)


def spectrum(table_in, signal):
    return jnp.einsum("kfs,sc->kfc", table_in, signal, precision=FULL_PRECISION)


def sample_spectrum(table_pair, signal):
    upper_term = jnp.einsum(
        "kfs,sc->kfc", table_pair[0], signal, preferred_element_type=jnp.float32
    )
    lower_term = jnp.einsum(
        "kfs,sc->kfc", table_pair[1], signal, preferred_element_type=jnp.float32
    )
    return upper_term + lower_term


def sample_pullback(table_pair, signal):
    upper_term = jnp.einsum(
        "ksf,sc->kfc", table_pair[0], signal, preferred_element_type=jnp.float32
    )
    lower_term = jnp.einsum(
        "ksf,sc->kfc", table_pair[1], signal, preferred_element_type=jnp.float32
    )
    return upper_term + lower_term


def complex_product(left_factor, right_factor):
    real_part = left_factor[0] * right_factor[0] - left_factor[1] * right_factor[1]
    imag_part = left_factor[0] * right_factor[1] + left_factor[1] * right_factor[0]
    return jnp.stack([real_part, imag_part])


def conjugate_product(left_factor, right_factor):
    real_part = left_factor[0] * right_factor[0] + left_factor[1] * right_factor[1]
    imag_part = left_factor[1] * right_factor[0] - left_factor[0] * right_factor[1]
    return jnp.stack([real_part, imag_part])


def weighted_sum(filter_mixes, spectra_items):
    accumulated = complex_product(filter_mixes[0], spectra_items[0])
    for offset in range(1, len(filter_mixes)):
        accumulated = accumulated + complex_product(filter_mixes[offset], spectra_items[offset])
    return accumulated


def per_device(
    inputs,
    gate_values,
    grad_out,
    first_weight,
    first_bias,
    second_weight,
    second_bias,
    out_weight,
    decay_rates,
    mask_lengths,
):
    shard_rows = inputs.shape[0]
    window = SPAN * shard_rows
    front_table, mirror_table, back_plain, back_table, mirror_out, fold_table, parity = (
        transform_tables(shard_rows)
    )
    front_pair = split_table(front_table)
    mirror_pair = split_table(mirror_table)
    pull_pair = split_table(back_plain)
    features = lag_features(window, first_weight.shape[0])
    pre_first = jnp.dot(features, first_weight, precision=FULL_PRECISION) + first_bias
    hidden_one = jnp.sin(pre_first)
    pre_second = jnp.dot(hidden_one, second_weight, precision=FULL_PRECISION) + second_bias
    hidden_two = jnp.sin(pre_second)
    lag_index = jnp.arange(window, dtype=jnp.int32)
    envelope = jnp.exp(-decay_rates[None, :] * lag_index.astype(jnp.float32)[:, None]) * (
        lag_index[:, None] < mask_lengths[None, :]
    ).astype(jnp.float32)
    filter_taps = jnp.dot(hidden_two, out_weight, precision=FULL_PRECISION) * envelope
    block_spectra = [
        spectrum(front_table, filter_taps[block * shard_rows : (block + 1) * shard_rows])
        for block in range(SPAN)
    ]
    filter_mixes = []
    for offset in range(SPAN + 1):
        if offset == 0:
            mixed = parity * block_spectra[0]
        elif offset == SPAN:
            mixed = block_spectra[SPAN - 1]
        else:
            mixed = block_spectra[offset - 1] + parity * block_spectra[offset]
        filter_mixes.append(mixed)
    carried = (grad_out.astype(jnp.float32) * gate_values.astype(jnp.float32)).astype(jnp.bfloat16)
    earlier_spectra = [sample_spectrum(front_pair, inputs)]
    later_spectra = [sample_spectrum(mirror_pair, carried)]
    for offset in range(1, SPAN + 1):
        earlier = passed_along(inputs, "seq", offset)
        later = passed_along(carried, "seq", -offset)
        earlier_spectra.append(sample_spectrum(front_pair, earlier))
        later_spectra.append(sample_spectrum(mirror_pair, later))
    convolved = jnp.einsum(
        "ksf,kfc->sc",
        back_table,
        weighted_sum(filter_mixes, earlier_spectra),
        precision=FULL_PRECISION,
    )
    grad_gates = (grad_out.astype(jnp.float32) * convolved).astype(jnp.bfloat16)
    grad_inputs = jnp.einsum(
        "ksf,kfc->sc",
        mirror_out,
        weighted_sum(filter_mixes, later_spectra),
        precision=FULL_PRECISION,
    ).astype(jnp.bfloat16)
    pulled = sample_pullback(pull_pair, carried)
    grad_mixes = [conjugate_product(pulled, spectra_item) for spectra_item in earlier_spectra]
    pieces = []
    for block in range(SPAN):
        grad_block = parity * grad_mixes[block] + grad_mixes[block + 1]
        pieces.append(jnp.einsum("kfs,kfc->sc", fold_table, grad_block, precision=FULL_PRECISION))
    tap_terms = jnp.concatenate(pieces, axis=0)
    grad_scale = 1.0 / math.sqrt(lax.axis_size("seq") * shard_rows * window)
    tap_sums = lax.psum(tap_terms, "seq")
    grad_taps = tap_sums * envelope * grad_scale
    grad_out_weight = jnp.dot(hidden_two.T, grad_taps, precision=FULL_PRECISION)
    unit_grad = lax.psum(
        jnp.dot(grad_taps, out_weight.T, precision=FULL_PRECISION).astype(jnp.bfloat16), "ch"
    ).astype(jnp.float32)
    grad_two = unit_grad * jnp.cos(pre_second)
    grad_second_weight = jnp.dot(hidden_one.T, grad_two, precision=FULL_PRECISION)
    grad_second_bias = jnp.sum(grad_two, axis=0)
    grad_one = jnp.dot(grad_two, second_weight.T, precision=FULL_PRECISION) * jnp.cos(pre_first)
    grad_first_weight = jnp.dot(features.T, grad_one, precision=FULL_PRECISION)
    grad_first_bias = jnp.sum(grad_one, axis=0)
    return (
        grad_inputs,
        grad_gates,
        grad_first_weight,
        grad_first_bias,
        grad_second_weight,
        grad_second_bias,
        grad_out_weight,
    )


VMEM_LIMIT = 40_000_000
DRAIN_LIMIT = 8_000_000
EARLY, MIDDLE = 3, 5
MESH = pl.DeviceIdType.MESH


def bf(value):
    return value.astype(jnp.bfloat16)


def dot(left, right, dims=((1,), (0,)), precision=None):
    return lax.dot_general(
        left, right, (dims, ((), ())), precision=precision, preferred_element_type=jnp.float32
    )


def packed_table(tokens):
    half = tokens // 2
    freq = np.arange(half)[:, None]
    time = np.arange(tokens)[None, :]
    angles = 2.0 * np.pi / tokens * (freq * time % tokens)
    lower = -np.sin(angles)
    lower[0] = 1.0 - 2.0 * (np.arange(tokens) % 2)
    return np.concatenate([np.cos(angles), lower]).astype(np.float32)


def exchange_kernel(
    sizes, x_hbm, gate_hbm, gout_hbm, w1_hbm, b1_hbm, w2_hbm, b2_hbm, decay_hbm, mask_hbm,
    feat_hbm, featt_hbm, ow_hbm, table_hbm, turned_hbm,
    gi_ref, gg_ref, gw1_ref, gb1_ref, gw2_ref, gb2_ref, gow_ref,
    gate_ref, gout_ref, w1_ref, b1_ref, w2_ref, b2_ref, decay_ref, mask_ref,
    feat_ref, featt_ref, ow, table, turned,
    ow_turned, carried, xs, cs, conv_in, taps, env, xspec, cspec, tspec, prod_v, prod_t,
    prod_g, back_v, back_g, sums, gts, gtall, units, send_sem, recv_sem, usend, urecv,
    local_sem, late_sem,
):
    n, m, rows, width, window, period = sizes
    tokens = n * rows
    half = tokens // 2
    side = n // 2
    me = lax.axis_index("seq")
    mine = lax.axis_index("ch")
    early = n // 4
    late = n - early
    steps = range(1, n)
    others = {step: lax.rem(mine + step, m) for step in range(1, m)}
    last = me >= late
    base_peer = me // side * side
    near = [base_peer + lax.rem(me - base_peer + step, side) for step in range(1, side)]
    across = lax.rem(me + side, n)
    far = [side - base_peer + lax.rem(me - base_peer + step, side) for step in range(side)]

    barrier = pltpu.get_barrier_semaphore()

    def greet(peer):
        pl.semaphore_signal(barrier, inc=1, device_id={"seq": peer}, device_id_type=MESH)

    for at in range(late, n):
        @pl.when(me != at)
        def _():
            greet(at)

    @pl.when(jnp.logical_not(last))
    def _():
        for step in range(1, late):
            greet(lax.rem(me + step, late))

    for step in range(1, m):
        pl.semaphore_signal(barrier, inc=1, device_id={"ch": others[step]}, device_id_type=MESH)

    own_rows = pl.ds(pl.multiple_of(me * rows, rows), rows)
    own_cols = pl.ds(pl.multiple_of(me * width, width), width)
    loads = []
    for at, (source, target) in enumerate((
        (gate_hbm, gate_ref), (gout_hbm, gout_ref), (x_hbm.at[:, own_cols], xs.at[own_rows, :]),
        (w1_hbm, w1_ref), (b1_hbm, b1_ref), (w2_hbm, w2_ref), (b2_hbm, b2_ref),
        (decay_hbm, decay_ref), (mask_hbm, mask_ref), (feat_hbm, feat_ref),
        (featt_hbm, featt_ref), (ow_hbm, ow), (table_hbm, table), (turned_hbm, turned),
    )):
        load = pltpu.make_async_copy(source, target, local_sem.at[at])
        load.start()
        loads.append(load)
    pl.semaphore_wait(barrier, jnp.where(last, n - 1, late - 1) + m - 1)

    @pl.when(last)
    def _():
        for at in range(late):
            pl.semaphore_signal(late_sem, inc=1, device_id={"seq": at}, device_id_type=MESH)

    def move(kind, step, source, target):
        return pltpu.make_async_remote_copy(
            src_ref=source, dst_ref=target,
            send_sem=send_sem.at[kind, step], recv_sem=recv_sem.at[kind, step],
            device_id={"seq": lax.rem(me + step, n)}, device_id_type=MESH,
        )

    def ahead(peer):
        return lax.rem(peer - me + n, n)

    def columns(peer):
        return pl.ds(pl.multiple_of(peer * width, width), width)

    def block(peer):
        return pl.ds(pl.multiple_of(peer * rows, rows), rows)

    x_moves = [move(0, step, xs.at[own_rows, :], xs.at[own_rows, :]) for step in steps]
    c_moves = [move(1, step, cs.at[own_rows, :], cs.at[own_rows, :]) for step in steps]
    for at in range(n - 1):
        around = lax.rem(me + 1 + at, n)
        ahead_of = lax.rem(me + 1 + at, late) if at < late - 1 else at + 1
        peer = jnp.where(last, around, ahead_of)
        if at == late - 1:

            @pl.when(jnp.logical_not(last))
            def _():
                pl.semaphore_wait(late_sem, n - late)

        move(0, ahead(peer), x_hbm.at[:, columns(peer)], xs.at[own_rows, :]).start()
    for load in loads[:2]:
        load.wait()
    carried[...] = bf(gout_ref[...].astype(jnp.float32) * gate_ref[...].astype(jnp.float32))
    for step in steps:
        peer = lax.rem(me + step, n)
        move(1, step, carried.at[:, columns(peer)], cs.at[own_rows, :]).start()
    cs[own_rows, :] = carried[:, own_cols]

    full = lax.Precision.HIGHEST
    for load in loads[2:]:
        load.wait()
    pre_one = dot(feat_ref[...], w1_ref[...], precision=full) + b1_ref[...]
    h_one = jnp.sin(pre_one)
    slope_one = jnp.cos(pre_one)
    pre_two = dot(h_one, w2_ref[...], precision=full) + b2_ref[...]
    h_two = jnp.sin(pre_two)
    slope_two = jnp.cos(pre_two)
    base = dot(h_two, ow[:, own_cols], precision=full)
    decay = decay_ref[:, own_cols]
    lengths = mask_ref[:, own_cols]
    for at in range(window // period):
        lag = lax.broadcasted_iota(jnp.int32, (period, width), 0) + at * period
        part = jnp.where(lag < lengths, jnp.exp(-decay * lag.astype(jnp.float32)), 0.0)
        env[pl.ds(at * period, period), :] = part
        taps[pl.ds(at * period, period), :] = bf(base * part)

    tspec[...] = dot(table[:, 0:window], taps[...])

    h_one_t = bf(h_one.T)
    w2_turned = bf(w2_ref[...].T)
    featt = bf(featt_ref[...])
    ow_turned[...] = bf(ow[...].T)
    h_two_t = bf(h_two.T)

    def parts(i):
        upper = pl.ds(pl.multiple_of(i * 64, 64), 64)
        lower = pl.ds(pl.multiple_of(half + i * 64, 64), 64)
        first = (lax.broadcasted_iota(jnp.int32, (64, width), 0) + i * 64) == 0
        weight = jnp.where(first, 1.0 / tokens, 2.0 / tokens)
        return upper, lower, first, weight

    for copy in x_moves:
        copy.wait_recv()

    xspec[...] = dot(table[...], xs[...])

    @pl.loop(0, half // 64)
    def _(i):
        upper, lower, first, weight = parts(i)
        xr, xi = xspec[upper, :], xspec[lower, :]
        hr, hi = tspec[upper, :], tspec[lower, :]
        hx = hi * xi
        prod_v[upper, :] = bf((hr * xr - jnp.where(first, 0.0, hx)) * weight)
        prod_v[lower, :] = bf(jnp.where(first, hx, hr * xi + hi * xr) * weight)

    back_v[...] = bf(dot(turned[...], prod_v[...]))

    v_moves = [
        move(2, step, back_v.at[own_rows, :], conv_in.at[:, own_cols]) for step in steps
    ]

    def send_conv(some):
        for step in some:
            peer = lax.rem(me + step, n)
            move(2, step, back_v.at[block(peer), :], conv_in.at[:, own_cols]).start()

    send_conv(steps[:EARLY])
    conv_in[:, own_cols] = back_v[own_rows, :]

    for copy in c_moves:
        copy.wait_recv()

    cspec[...] = dot(table[...], cs[...])

    @pl.loop(0, half // 64)
    def _(i):
        upper, lower, first, weight = parts(i)
        xr, xi = xspec[upper, :], xspec[lower, :]
        cr, ci = cspec[upper, :], cspec[lower, :]
        cx = ci * xi
        prod_t[upper, :] = bf((cr * xr + jnp.where(first, 0.0, cx)) * weight)
        prod_t[lower, :] = bf(jnp.where(first, cx, ci * xr - cr * xi) * weight)

    sums[...] = dot(turned[0:window, :], prod_t[...])

    folded = sums[0:period, :] * env[0:period, :]
    for at in range(1, window // period):
        piece = pl.ds(at * period, period)
        folded = folded + sums[piece, :] * env[piece, :]
    folded = bf(folded * (1.0 / math.sqrt(tokens * window)))
    gts[...] = folded
    gtall[:, own_cols] = folded

    def give(peer):
        return move(4, ahead(peer), gts, gtall.at[:, own_cols])

    def taken(kind, peer):
        return move(kind, lax.rem(me - peer + n, n), gts, gtall.at[:, own_cols])

    give(across).start()
    for at in range(early):
        @pl.when((me >= side) & (across != at))
        def _():
            give(at).start()


    for peer in near:
        give(peer).start()
    send_conv(steps[EARLY:MIDDLE])

    @pl.loop(0, half // 64)
    def _(i):
        upper, lower, first, weight = parts(i)
        cr, ci = cspec[upper, :], cspec[lower, :]
        hr, hi = tspec[upper, :], tspec[lower, :]
        hc = hi * ci
        prod_g[upper, :] = bf((hr * cr + jnp.where(first, 0.0, hc)) * weight)
        prod_g[lower, :] = bf(jnp.where(first, hc, hr * ci - hi * cr) * weight)

    back_g[...] = bf(dot(turned[...], prod_g[...]))


    def forward(peer):
        return move(5, ahead(peer), gtall.at[:, columns(across)], gtall.at[:, columns(across)])

    taken(4, across).wait_recv()

    @pl.when(me >= side)
    def _():
        for peer in near:
            forward(peer).start()

    for at in range(early, side):
        @pl.when((me < side) & (me != at))
        def _():
            forward(at).start()


    send_conv(steps[MIDDLE:])
    g_moves = [move(3, step, back_g.at[own_rows, :], gi_ref.at[:, own_cols]) for step in steps]
    for at in range(n - 1):
        peer = at + (me <= at).astype(jnp.int32)
        move(3, ahead(peer), back_g.at[block(peer), :], gi_ref.at[:, own_cols]).start()
    gi_ref[:, own_cols] = back_g[own_rows, :]
    for peer in near:
        taken(4, peer).wait_recv()

    @pl.when(me >= side)
    def _():
        for peer in near:
            taken(5, peer).wait_recv()

    @pl.when(me < early)
    def _():
        for peer in far[1:]:
            taken(4, peer).wait_recv()

    @pl.when((me >= early) & (me < side))
    def _():
        for at in range(early):
            taken(5, at).wait_recv()
        for step in range(1, side - early):
            taken(5, early + lax.rem(me - early + step, side - early)).wait_recv()


    units[mine] = bf(dot(gtall[...], ow_turned[...]))
    crossing = []
    for step in range(1, m):
        copy = pltpu.make_async_remote_copy(
            src_ref=units.at[mine], dst_ref=units.at[mine],
            send_sem=usend.at[step], recv_sem=urecv.at[step],
            device_id={"ch": others[step]}, device_id_type=MESH,
        )
        copy.start()
        crossing.append(copy)
    gow_ref[...] = dot(h_two_t, gtall[...])
    for copy in v_moves:
        copy.wait_recv()
    gg_ref[...] = bf(gout_ref[...].astype(jnp.float32) * conv_in[...].astype(jnp.float32))
    for copy in crossing:
        copy.wait_recv()
    unit = units[0].astype(jnp.float32)
    for other in range(1, m):
        unit = unit + units[other].astype(jnp.float32)
    grad_two = unit * slope_two
    narrow_two = bf(grad_two)
    grad_one = dot(narrow_two, w2_turned) * slope_one
    gw1_ref[...] = dot(featt, bf(grad_one))
    gw2_ref[...] = dot(h_one_t, narrow_two)
    gb2_ref[...] = jnp.sum(grad_two, axis=0, keepdims=True)
    gb1_ref[...] = jnp.sum(grad_one, axis=0, keepdims=True)
    for copy in x_moves + c_moves + v_moves:
        copy.wait_send()
    for peer in near:
        give(peer).wait_send()

    give(across).wait_send()
    for at in range(early):
        @pl.when((me >= side) & (across != at))
        def _():
            give(at).wait_send()

    @pl.when(me >= side)
    def _():
        for peer in near:
            forward(peer).wait_send()

    for at in range(early, side):
        @pl.when((me < side) & (me != at))
        def _():
            forward(at).wait_send()

    for copy in crossing:
        copy.wait_send()
    for copy in g_moves:
        copy.wait()


def drain_kernel(*refs):
    count = len(refs) // 2
    store_sem = refs[-1]
    stores = [
        pltpu.make_async_copy(refs[at], refs[count + at], store_sem.at[at])
        for at in range(count)
    ]
    for copy in stores:
        copy.start()
    for copy in stores:
        copy.wait()


def exchanged(
    mesh_shape, inputs, gate_values, grad_out, first_weight, first_bias, second_weight,
    second_bias, out_weight, decay_rates, mask_lengths,
):
    n, m = mesh_shape["seq"], mesh_shape["ch"]
    rows, channels = inputs.shape
    width = channels // n
    window = SPAN * rows
    emb, units = first_weight.shape
    period = 2 * emb
    tokens = n * rows
    angles = (
        2.0 * np.pi / period
        * (np.arange(period)[:, None] * (np.arange(emb // 2)[None, :] + 1) % period)
    )
    features = np.concatenate([np.cos(angles), np.sin(angles)], axis=1).astype(np.float32)
    f32, b16 = jnp.float32, jnp.bfloat16
    outside = pl.BlockSpec(memory_space=pltpu.HBM)
    inside = pl.BlockSpec(memory_space=pltpu.VMEM)
    shape = jax.ShapeDtypeStruct
    sem = pltpu.SemaphoreType.DMA
    table = packed_table(tokens)
    staged = (
        gate_values, grad_out, first_weight, first_bias[None], second_weight,
        second_bias[None], decay_rates[None], mask_lengths[None],
        jnp.asarray(features), jnp.asarray(features.T.copy()), out_weight,
        jnp.asarray(table, dtype=b16), jnp.asarray(table.T.copy(), dtype=b16),
    )
    out_shapes = (
        shape((rows, channels), b16), shape((rows, channels), b16),
        shape((emb, units), f32), shape((1, units), f32),
        shape((units, units), f32), shape((1, units), f32),
        shape((units, channels), f32),
    )
    outs = pl.pallas_call(
        functools.partial(exchange_kernel, (n, m, rows, width, window, period)),
        out_shape=tuple(pltpu.VMEM(out.shape, out.dtype) for out in out_shapes),
        in_specs=[outside] * 14,
        out_specs=(inside,) * 7,
        scratch_shapes=[
            *[pltpu.VMEM(array.shape, array.dtype) for array in staged],
            pltpu.VMEM((channels, units), b16),
            pltpu.VMEM((rows, channels), b16),
            pltpu.VMEM((tokens, width), b16), pltpu.VMEM((tokens, width), b16),
            pltpu.VMEM((rows, channels), b16),
            pltpu.VMEM((window, width), b16), pltpu.VMEM((window, width), f32),
            pltpu.VMEM((tokens, width), f32), pltpu.VMEM((tokens, width), f32),
            pltpu.VMEM((tokens, width), f32),
            pltpu.VMEM((tokens, width), b16), pltpu.VMEM((tokens, width), b16),
            pltpu.VMEM((tokens, width), b16),
            pltpu.VMEM((tokens, width), b16), pltpu.VMEM((tokens, width), b16),
            pltpu.VMEM((window, width), f32),
            pltpu.VMEM((period, width), b16), pltpu.VMEM((period, channels), b16),
            pltpu.VMEM((m, period, units), b16),
            sem((6, n)), sem((6, n)), sem((m,)), sem((m,)), sem((14,)),
            pltpu.SemaphoreType.REGULAR,
        ],
        compiler_params=pltpu.CompilerParams(
            collective_id=0, has_side_effects=True, vmem_limit_bytes=VMEM_LIMIT
        ),
        name="exchange",
    )(*[pltpu.with_memory_space_constraint(array, pltpu.HBM) for array in (inputs, *staged)])
    outs = pl.pallas_call(
        drain_kernel,
        out_shape=out_shapes,
        in_specs=[inside] * 7,
        out_specs=(outside,) * 7,
        scratch_shapes=[sem((7,))],
        compiler_params=pltpu.CompilerParams(vmem_limit_bytes=DRAIN_LIMIT),
        name="drain",
    )(*outs)
    grad_in, gates, gw1, gb1, gw2, gb2, gow = outs
    return grad_in, gates, gw1, gb1[0], gw2, gb2[0], gow


def solution(mesh):
    def body(*arrays):
        rows, channels = arrays[0].shape
        count = mesh.shape["seq"]
        fits = channels == 128 * count and rows % 128 == 0 and count == 2 * SPAN
        if fits:
            return exchanged(mesh.shape, *arrays)
        return per_device(*arrays)

    in_specs = (
        P("seq", "ch"),
        P("seq", "ch"),
        P("seq", "ch"),
        P(),
        P(),
        P(),
        P(),
        P(None, "ch"),
        P("ch"),
        P("ch"),
    )
    out_specs = (P("seq", "ch"), P("seq", "ch"), P(), P(), P(), P(), P(None, "ch"))
    return jax.shard_map(
        body, mesh=mesh, in_specs=in_specs, out_specs=out_specs, check_vma=False
    )
```

```python
import math

import jax
import jax.numpy as jnp
import functools

import numpy as np
from jax import lax
from jax.experimental import pallas as pl
from jax.experimental.pallas import tpu as pltpu
from jax.sharding import PartitionSpec as P

SPAN = 4


FULL_PRECISION = lax.Precision.HIGHEST


def passed_along(value, axis, steps):
    count = lax.axis_size(axis)
    pairs = [(source, (source + steps) % count) for source in range(count)]
    return lax.ppermute(value, axis, pairs)


def angle_table(first_index, second_index, period):
    product = first_index[:, None] * second_index[None, :] % period
    return 2.0 * math.pi / period * product.astype(jnp.float32)


def lag_features(lag_count, feature_count):
    lag_index = jnp.arange(lag_count, dtype=jnp.int32)
    band_index = jnp.arange(feature_count // 2, dtype=jnp.int32) + 1
    phases = angle_table(lag_index, band_index, 2 * feature_count)
    return jnp.concatenate([jnp.cos(phases), jnp.sin(phases)], axis=1)


def split_table(table):
    upper_part = table.astype(jnp.bfloat16)
    lower_part = (table - upper_part.astype(jnp.float32)).astype(jnp.bfloat16)
    return (upper_part, lower_part)


def transform_tables(shard_rows):
    period = 2 * shard_rows
    frequency = jnp.arange(shard_rows + 1, dtype=jnp.int32)
    position = jnp.arange(shard_rows, dtype=jnp.int32)
    bin_weight = jnp.where((frequency == 0) | (frequency == shard_rows), 1.0, 2.0).astype(
        jnp.float32
    )
    forward_angles = angle_table(frequency, position, period)
    mirror_angles = angle_table(frequency, shard_rows - 1 - position, period)
    back_angles = angle_table(position + shard_rows, frequency, period)
    mirror_back = angle_table(2 * shard_rows - 1 - position, frequency, period)
    front_table = jnp.stack([jnp.cos(forward_angles), -jnp.sin(forward_angles)])
    mirror_table = jnp.stack([jnp.cos(mirror_angles), -jnp.sin(mirror_angles)])
    back_plain = jnp.stack([jnp.cos(back_angles), -jnp.sin(back_angles)]) / period
    back_table = back_plain * bin_weight[None, None, :]
    mirror_out = jnp.stack([jnp.cos(mirror_back), -jnp.sin(mirror_back)]) * (
        bin_weight[None, None, :] / period
    )
    fold_table = front_table * bin_weight[None, :, None]
    parity = (1.0 - 2.0 * (frequency % 2).astype(jnp.float32))[None, :, None]
    return (front_table, mirror_table, back_plain, back_table, mirror_out, fold_table, parity)


def spectrum(table_in, signal):
    return jnp.einsum("kfs,sc->kfc", table_in, signal, precision=FULL_PRECISION)


def sample_spectrum(table_pair, signal):
    upper_term = jnp.einsum(
        "kfs,sc->kfc", table_pair[0], signal, preferred_element_type=jnp.float32
    )
    lower_term = jnp.einsum(
        "kfs,sc->kfc", table_pair[1], signal, preferred_element_type=jnp.float32
    )
    return upper_term + lower_term


def sample_pullback(table_pair, signal):
    upper_term = jnp.einsum(
        "ksf,sc->kfc", table_pair[0], signal, preferred_element_type=jnp.float32
    )
    lower_term = jnp.einsum(
        "ksf,sc->kfc", table_pair[1], signal, preferred_element_type=jnp.float32
    )
    return upper_term + lower_term


def complex_product(left_factor, right_factor):
    real_part = left_factor[0] * right_factor[0] - left_factor[1] * right_factor[1]
    imag_part = left_factor[0] * right_factor[1] + left_factor[1] * right_factor[0]
    return jnp.stack([real_part, imag_part])


def conjugate_product(left_factor, right_factor):
    real_part = left_factor[0] * right_factor[0] + left_factor[1] * right_factor[1]
    imag_part = left_factor[1] * right_factor[0] - left_factor[0] * right_factor[1]
    return jnp.stack([real_part, imag_part])


def weighted_sum(filter_mixes, spectra_items):
    accumulated = complex_product(filter_mixes[0], spectra_items[0])
    for offset in range(1, len(filter_mixes)):
        accumulated = accumulated + complex_product(filter_mixes[offset], spectra_items[offset])
    return accumulated


def per_device(
    inputs,
    gate_values,
    grad_out,
    first_weight,
    first_bias,
    second_weight,
    second_bias,
    out_weight,
    decay_rates,
    mask_lengths,
):
    shard_rows = inputs.shape[0]
    window = SPAN * shard_rows
    front_table, mirror_table, back_plain, back_table, mirror_out, fold_table, parity = (
        transform_tables(shard_rows)
    )
    front_pair = split_table(front_table)
    mirror_pair = split_table(mirror_table)
    pull_pair = split_table(back_plain)
    features = lag_features(window, first_weight.shape[0])
    pre_first = jnp.dot(features, first_weight, precision=FULL_PRECISION) + first_bias
    hidden_one = jnp.sin(pre_first)
    pre_second = jnp.dot(hidden_one, second_weight, precision=FULL_PRECISION) + second_bias
    hidden_two = jnp.sin(pre_second)
    lag_index = jnp.arange(window, dtype=jnp.int32)
    envelope = jnp.exp(-decay_rates[None, :] * lag_index.astype(jnp.float32)[:, None]) * (
        lag_index[:, None] < mask_lengths[None, :]
    ).astype(jnp.float32)
    filter_taps = jnp.dot(hidden_two, out_weight, precision=FULL_PRECISION) * envelope
    block_spectra = [
        spectrum(front_table, filter_taps[block * shard_rows : (block + 1) * shard_rows])
        for block in range(SPAN)
    ]
    filter_mixes = []
    for offset in range(SPAN + 1):
        if offset == 0:
            mixed = parity * block_spectra[0]
        elif offset == SPAN:
            mixed = block_spectra[SPAN - 1]
        else:
            mixed = block_spectra[offset - 1] + parity * block_spectra[offset]
        filter_mixes.append(mixed)
    carried = (grad_out.astype(jnp.float32) * gate_values.astype(jnp.float32)).astype(jnp.bfloat16)
    earlier_spectra = [sample_spectrum(front_pair, inputs)]
    later_spectra = [sample_spectrum(mirror_pair, carried)]
    for offset in range(1, SPAN + 1):
        earlier = passed_along(inputs, "seq", offset)
        later = passed_along(carried, "seq", -offset)
        earlier_spectra.append(sample_spectrum(front_pair, earlier))
        later_spectra.append(sample_spectrum(mirror_pair, later))
    convolved = jnp.einsum(
        "ksf,kfc->sc",
        back_table,
        weighted_sum(filter_mixes, earlier_spectra),
        precision=FULL_PRECISION,
    )
    grad_gates = (grad_out.astype(jnp.float32) * convolved).astype(jnp.bfloat16)
    grad_inputs = jnp.einsum(
        "ksf,kfc->sc",
        mirror_out,
        weighted_sum(filter_mixes, later_spectra),
        precision=FULL_PRECISION,
    ).astype(jnp.bfloat16)
    pulled = sample_pullback(pull_pair, carried)
    grad_mixes = [conjugate_product(pulled, spectra_item) for spectra_item in earlier_spectra]
    pieces = []
    for block in range(SPAN):
        grad_block = parity * grad_mixes[block] + grad_mixes[block + 1]
        pieces.append(jnp.einsum("kfs,kfc->sc", fold_table, grad_block, precision=FULL_PRECISION))
    tap_terms = jnp.concatenate(pieces, axis=0)
    grad_scale = 1.0 / math.sqrt(lax.axis_size("seq") * shard_rows * window)
    tap_sums = lax.psum(tap_terms, "seq")
    grad_taps = tap_sums * envelope * grad_scale
    grad_out_weight = jnp.dot(hidden_two.T, grad_taps, precision=FULL_PRECISION)
    unit_grad = lax.psum(
        jnp.dot(grad_taps, out_weight.T, precision=FULL_PRECISION).astype(jnp.bfloat16), "ch"
    ).astype(jnp.float32)
    grad_two = unit_grad * jnp.cos(pre_second)
    grad_second_weight = jnp.dot(hidden_one.T, grad_two, precision=FULL_PRECISION)
    grad_second_bias = jnp.sum(grad_two, axis=0)
    grad_one = jnp.dot(grad_two, second_weight.T, precision=FULL_PRECISION) * jnp.cos(pre_first)
    grad_first_weight = jnp.dot(features.T, grad_one, precision=FULL_PRECISION)
    grad_first_bias = jnp.sum(grad_one, axis=0)
    return (
        grad_inputs,
        grad_gates,
        grad_first_weight,
        grad_first_bias,
        grad_second_weight,
        grad_second_bias,
        grad_out_weight,
    )


VMEM_LIMIT = 40_000_000
DRAIN_LIMIT = 8_000_000
EARLY, MIDDLE = 3, 5
MESH = pl.DeviceIdType.MESH


def bf(value):
    return value.astype(jnp.bfloat16)


def dot(left, right, dims=((1,), (0,)), precision=None):
    return lax.dot_general(
        left, right, (dims, ((), ())), precision=precision, preferred_element_type=jnp.float32
    )


def packed_table(tokens):
    half = tokens // 2
    freq = np.arange(half)[:, None]
    time = np.arange(tokens)[None, :]
    angles = 2.0 * np.pi / tokens * (freq * time % tokens)
    lower = -np.sin(angles)
    lower[0] = 1.0 - 2.0 * (np.arange(tokens) % 2)
    return np.concatenate([np.cos(angles), lower]).astype(np.float32)


def exchange_kernel(
    sizes, x_hbm, gate_hbm, gout_hbm, w1_hbm, b1_hbm, w2_hbm, b2_hbm, decay_hbm, mask_hbm,
    feat_hbm, featt_hbm, ow_hbm, table_hbm, turned_hbm,
    gi_ref, gg_ref, gw1_ref, gb1_ref, gw2_ref, gb2_ref, gow_ref,
    gate_ref, gout_ref, w1_ref, b1_ref, w2_ref, b2_ref, decay_ref, mask_ref,
    feat_ref, featt_ref, ow, table, turned,
    ow_turned, carried, xs, cs, conv_in, taps, env, xspec, cspec, tspec, prod_v, prod_t,
    prod_g, back_v, back_g, sums, gts, gtall, units, send_sem, recv_sem, usend, urecv,
    local_sem, late_sem,
):
    n, m, rows, width, window, period = sizes
    tokens = n * rows
    half = tokens // 2
    side = n // 2
    me = lax.axis_index("seq")
    mine = lax.axis_index("ch")
    early = n // 4
    late = n - early
    steps = range(1, n)
    others = {step: lax.rem(mine + step, m) for step in range(1, m)}
    last = me >= late
    base_peer = me // side * side
    near = [base_peer + lax.rem(me - base_peer + step, side) for step in range(1, side)]
    across = lax.rem(me + side, n)
    far = [side - base_peer + lax.rem(me - base_peer + step, side) for step in range(side)]

    barrier = pltpu.get_barrier_semaphore()

    def greet(peer):
        pl.semaphore_signal(barrier, inc=1, device_id={"seq": peer}, device_id_type=MESH)

    for at in range(late, n):
        @pl.when(me != at)
        def _():
            greet(at)

    @pl.when(jnp.logical_not(last))
    def _():
        for step in range(1, late):
            greet(lax.rem(me + step, late))

    for step in range(1, m):
        pl.semaphore_signal(barrier, inc=1, device_id={"ch": others[step]}, device_id_type=MESH)

    own_rows = pl.ds(pl.multiple_of(me * rows, rows), rows)
    own_cols = pl.ds(pl.multiple_of(me * width, width), width)
    loads = []
    for at, (source, target) in enumerate((
        (gate_hbm, gate_ref), (gout_hbm, gout_ref), (x_hbm.at[:, own_cols], xs.at[own_rows, :]),
        (w1_hbm, w1_ref), (b1_hbm, b1_ref), (w2_hbm, w2_ref), (b2_hbm, b2_ref),
        (decay_hbm, decay_ref), (mask_hbm, mask_ref), (feat_hbm, feat_ref),
        (featt_hbm, featt_ref), (ow_hbm, ow), (table_hbm, table), (turned_hbm, turned),
    )):
        load = pltpu.make_async_copy(source, target, local_sem.at[at])
        load.start()
        loads.append(load)
    pl.semaphore_wait(barrier, jnp.where(last, n - 1, late - 1) + m - 1)

    @pl.when(last)
    def _():
        for at in range(late):
            pl.semaphore_signal(late_sem, inc=1, device_id={"seq": at}, device_id_type=MESH)

    def move(kind, step, source, target):
        return pltpu.make_async_remote_copy(
            src_ref=source, dst_ref=target,
            send_sem=send_sem.at[kind, step], recv_sem=recv_sem.at[kind, step],
            device_id={"seq": lax.rem(me + step, n)}, device_id_type=MESH,
        )

    def ahead(peer):
        return lax.rem(peer - me + n, n)

    def columns(peer):
        return pl.ds(pl.multiple_of(peer * width, width), width)

    def block(peer):
        return pl.ds(pl.multiple_of(peer * rows, rows), rows)

    x_moves = [move(0, step, xs.at[own_rows, :], xs.at[own_rows, :]) for step in steps]
    c_moves = [move(1, step, cs.at[own_rows, :], cs.at[own_rows, :]) for step in steps]
    for at in range(n - 1):
        around = lax.rem(me + 1 + at, n)
        ahead_of = lax.rem(me + 1 + at, late) if at < late - 1 else at + 1
        peer = jnp.where(last, around, ahead_of)
        if at == late - 1:

            @pl.when(jnp.logical_not(last))
            def _():
                pl.semaphore_wait(late_sem, n - late)

        move(0, ahead(peer), x_hbm.at[:, columns(peer)], xs.at[own_rows, :]).start()
    for load in loads[:2]:
        load.wait()
    carried[...] = bf(gout_ref[...].astype(jnp.float32) * gate_ref[...].astype(jnp.float32))
    for step in steps:
        peer = lax.rem(me + step, n)
        move(1, step, carried.at[:, columns(peer)], cs.at[own_rows, :]).start()
    cs[own_rows, :] = carried[:, own_cols]

    full = lax.Precision.HIGHEST
    for load in loads[2:]:
        load.wait()
    pre_one = dot(feat_ref[...], w1_ref[...], precision=full) + b1_ref[...]
    h_one = jnp.sin(pre_one)
    slope_one = jnp.cos(pre_one)
    pre_two = dot(h_one, w2_ref[...], precision=full) + b2_ref[...]
    h_two = jnp.sin(pre_two)
    slope_two = jnp.cos(pre_two)
    base = dot(h_two, ow[:, own_cols], precision=full)
    decay = decay_ref[:, own_cols]
    lengths = mask_ref[:, own_cols]
    for at in range(window // period):
        lag = lax.broadcasted_iota(jnp.int32, (period, width), 0) + at * period
        part = jnp.where(lag < lengths, jnp.exp(-decay * lag.astype(jnp.float32)), 0.0)
        env[pl.ds(at * period, period), :] = part
        taps[pl.ds(at * period, period), :] = bf(base * part)

    tspec[...] = dot(table[:, 0:window], taps[...])

    h_one_t = bf(h_one.T)
    w2_turned = bf(w2_ref[...].T)
    featt = bf(featt_ref[...])
    ow_turned[...] = bf(ow[...].T)
    h_two_t = bf(h_two.T)

    def parts(i):
        upper = pl.ds(pl.multiple_of(i * 64, 64), 64)
        lower = pl.ds(pl.multiple_of(half + i * 64, 64), 64)
        first = (lax.broadcasted_iota(jnp.int32, (64, width), 0) + i * 64) == 0
        weight = jnp.where(first, 1.0 / tokens, 2.0 / tokens)
        return upper, lower, first, weight

    for copy in x_moves:
        copy.wait_recv()

    xspec[...] = dot(table[...], xs[...])

    @pl.loop(0, half // 64)
    def _(i):
        upper, lower, first, weight = parts(i)
        xr, xi = xspec[upper, :], xspec[lower, :]
        hr, hi = tspec[upper, :], tspec[lower, :]
        hx = hi * xi
        prod_v[upper, :] = bf((hr * xr - jnp.where(first, 0.0, hx)) * weight)
        prod_v[lower, :] = bf(jnp.where(first, hx, hr * xi + hi * xr) * weight)

    back_v[...] = bf(dot(turned[...], prod_v[...]))

    v_moves = [
        move(2, step, back_v.at[own_rows, :], conv_in.at[:, own_cols]) for step in steps
    ]

    def send_conv(some):
        for step in some:
            peer = lax.rem(me + step, n)
            move(2, step, back_v.at[block(peer), :], conv_in.at[:, own_cols]).start()

    send_conv(steps[:EARLY])
    conv_in[:, own_cols] = back_v[own_rows, :]

    def arrived(kind, peer, target):
        move(kind, lax.rem(me - peer + n, n), target, target).wait_recv()

    near_span = pl.ds(pl.multiple_of(base_peer * rows, half), half)
    far_span = pl.ds(pl.multiple_of((side - base_peer) * rows, half), half)
    for peer in near:
        arrived(1, peer, cs.at[own_rows, :])
    cspec[...] = dot(table[:, near_span], cs[near_span, :])
    for peer in far:
        arrived(1, peer, cs.at[own_rows, :])
    cspec[...] += dot(table[:, far_span], cs[far_span, :])

    @pl.loop(0, half // 64)
    def _(i):
        upper, lower, first, weight = parts(i)
        xr, xi = xspec[upper, :], xspec[lower, :]
        cr, ci = cspec[upper, :], cspec[lower, :]
        cx = ci * xi
        prod_t[upper, :] = bf((cr * xr + jnp.where(first, 0.0, cx)) * weight)
        prod_t[lower, :] = bf(jnp.where(first, cx, ci * xr - cr * xi) * weight)

    sums[...] = dot(turned[0:window, :], prod_t[...])

    folded = sums[0:period, :] * env[0:period, :]
    for at in range(1, window // period):
        piece = pl.ds(at * period, period)
        folded = folded + sums[piece, :] * env[piece, :]
    folded = bf(folded * (1.0 / math.sqrt(tokens * window)))
    gts[...] = folded
    gtall[:, own_cols] = folded

    def give(peer):
        return move(4, ahead(peer), gts, gtall.at[:, own_cols])

    def taken(kind, peer):
        return move(kind, lax.rem(me - peer + n, n), gts, gtall.at[:, own_cols])

    give(across).start()
    for at in range(early):
        @pl.when((me >= side) & (across != at))
        def _():
            give(at).start()


    for peer in near:
        give(peer).start()
    send_conv(steps[EARLY:MIDDLE])

    @pl.loop(0, half // 64)
    def _(i):
        upper, lower, first, weight = parts(i)
        cr, ci = cspec[upper, :], cspec[lower, :]
        hr, hi = tspec[upper, :], tspec[lower, :]
        hc = hi * ci
        prod_g[upper, :] = bf((hr * cr + jnp.where(first, 0.0, hc)) * weight)
        prod_g[lower, :] = bf(jnp.where(first, hc, hr * ci - hi * cr) * weight)

    back_g[...] = bf(dot(turned[...], prod_g[...]))


    def forward(peer):
        return move(5, ahead(peer), gtall.at[:, columns(across)], gtall.at[:, columns(across)])

    taken(4, across).wait_recv()

    @pl.when(me >= side)
    def _():
        for peer in near:
            forward(peer).start()

    for at in range(early, side):
        @pl.when((me < side) & (me != at))
        def _():
            forward(at).start()


    g_moves = [move(3, step, back_g.at[own_rows, :], gi_ref.at[:, own_cols]) for step in steps]
    for at in range(n - 1):
        rising = at + (me <= at).astype(jnp.int32)
        peer = jnp.where(lax.rem(mine, 2) == 0, rising, lax.rem(me + 1 + at, n))
        move(3, ahead(peer), back_g.at[block(peer), :], gi_ref.at[:, own_cols]).start()
    send_conv(steps[MIDDLE:])
    gi_ref[:, own_cols] = back_g[own_rows, :]
    for peer in near:
        taken(4, peer).wait_recv()

    @pl.when(me >= side)
    def _():
        for peer in near:
            taken(5, peer).wait_recv()

    @pl.when(me < early)
    def _():
        for peer in far[1:]:
            taken(4, peer).wait_recv()

    @pl.when((me >= early) & (me < side))
    def _():
        for at in range(early):
            taken(5, at).wait_recv()
        for step in range(1, side - early):
            taken(5, early + lax.rem(me - early + step, side - early)).wait_recv()


    units[mine] = bf(dot(gtall[...], ow_turned[...]))
    crossing = []
    for step in range(1, m):
        copy = pltpu.make_async_remote_copy(
            src_ref=units.at[mine], dst_ref=units.at[mine],
            send_sem=usend.at[step], recv_sem=urecv.at[step],
            device_id={"ch": others[step]}, device_id_type=MESH,
        )
        copy.start()
        crossing.append(copy)
    gow_ref[...] = dot(h_two_t, gtall[...])
    for copy in v_moves:
        copy.wait_recv()
    gg_ref[...] = bf(gout_ref[...].astype(jnp.float32) * conv_in[...].astype(jnp.float32))
    for copy in crossing:
        copy.wait_recv()
    unit = units[0].astype(jnp.float32)
    for other in range(1, m):
        unit = unit + units[other].astype(jnp.float32)
    grad_two = unit * slope_two
    narrow_two = bf(grad_two)
    grad_one = dot(narrow_two, w2_turned) * slope_one
    gw1_ref[...] = dot(featt, bf(grad_one))
    gw2_ref[...] = dot(h_one_t, narrow_two)
    gb2_ref[...] = jnp.sum(grad_two, axis=0, keepdims=True)
    gb1_ref[...] = jnp.sum(grad_one, axis=0, keepdims=True)
    for copy in x_moves + c_moves + v_moves:
        copy.wait_send()
    for peer in near:
        give(peer).wait_send()

    give(across).wait_send()
    for at in range(early):
        @pl.when((me >= side) & (across != at))
        def _():
            give(at).wait_send()

    @pl.when(me >= side)
    def _():
        for peer in near:
            forward(peer).wait_send()

    for at in range(early, side):
        @pl.when((me < side) & (me != at))
        def _():
            forward(at).wait_send()

    for copy in crossing:
        copy.wait_send()
    for copy in g_moves:
        copy.wait()


def drain_kernel(*refs):
    count = len(refs) // 2
    store_sem = refs[-1]
    stores = [
        pltpu.make_async_copy(refs[at], refs[count + at], store_sem.at[at])
        for at in range(count)
    ]
    for copy in stores:
        copy.start()
    for copy in stores:
        copy.wait()


def exchanged(
    mesh_shape, inputs, gate_values, grad_out, first_weight, first_bias, second_weight,
    second_bias, out_weight, decay_rates, mask_lengths,
):
    n, m = mesh_shape["seq"], mesh_shape["ch"]
    rows, channels = inputs.shape
    width = channels // n
    window = SPAN * rows
    emb, units = first_weight.shape
    period = 2 * emb
    tokens = n * rows
    angles = (
        2.0 * np.pi / period
        * (np.arange(period)[:, None] * (np.arange(emb // 2)[None, :] + 1) % period)
    )
    features = np.concatenate([np.cos(angles), np.sin(angles)], axis=1).astype(np.float32)
    f32, b16 = jnp.float32, jnp.bfloat16
    outside = pl.BlockSpec(memory_space=pltpu.HBM)
    inside = pl.BlockSpec(memory_space=pltpu.VMEM)
    shape = jax.ShapeDtypeStruct
    sem = pltpu.SemaphoreType.DMA
    table = packed_table(tokens)
    staged = (
        gate_values, grad_out, first_weight, first_bias[None], second_weight,
        second_bias[None], decay_rates[None], mask_lengths[None],
        jnp.asarray(features), jnp.asarray(features.T.copy()), out_weight,
        jnp.asarray(table, dtype=b16), jnp.asarray(table.T.copy(), dtype=b16),
    )
    out_shapes = (
        shape((rows, channels), b16), shape((rows, channels), b16),
        shape((emb, units), f32), shape((1, units), f32),
        shape((units, units), f32), shape((1, units), f32),
        shape((units, channels), f32),
    )
    outs = pl.pallas_call(
        functools.partial(exchange_kernel, (n, m, rows, width, window, period)),
        out_shape=tuple(pltpu.VMEM(out.shape, out.dtype) for out in out_shapes),
        in_specs=[outside] * 14,
        out_specs=(inside,) * 7,
        scratch_shapes=[
            *[pltpu.VMEM(array.shape, array.dtype) for array in staged],
            pltpu.VMEM((channels, units), b16),
            pltpu.VMEM((rows, channels), b16),
            pltpu.VMEM((tokens, width), b16), pltpu.VMEM((tokens, width), b16),
            pltpu.VMEM((rows, channels), b16),
            pltpu.VMEM((window, width), b16), pltpu.VMEM((window, width), f32),
            pltpu.VMEM((tokens, width), f32), pltpu.VMEM((tokens, width), f32),
            pltpu.VMEM((tokens, width), f32),
            pltpu.VMEM((tokens, width), b16), pltpu.VMEM((tokens, width), b16),
            pltpu.VMEM((tokens, width), b16),
            pltpu.VMEM((tokens, width), b16), pltpu.VMEM((tokens, width), b16),
            pltpu.VMEM((window, width), f32),
            pltpu.VMEM((period, width), b16), pltpu.VMEM((period, channels), b16),
            pltpu.VMEM((m, period, units), b16),
            sem((6, n)), sem((6, n)), sem((m,)), sem((m,)), sem((14,)),
            pltpu.SemaphoreType.REGULAR,
        ],
        compiler_params=pltpu.CompilerParams(
            collective_id=0, has_side_effects=True, vmem_limit_bytes=VMEM_LIMIT
        ),
        name="exchange",
    )(*[pltpu.with_memory_space_constraint(array, pltpu.HBM) for array in (inputs, *staged)])
    outs = pl.pallas_call(
        drain_kernel,
        out_shape=out_shapes,
        in_specs=[inside] * 7,
        out_specs=(outside,) * 7,
        scratch_shapes=[sem((7,))],
        compiler_params=pltpu.CompilerParams(vmem_limit_bytes=DRAIN_LIMIT),
        name="drain",
    )(*outs)
    grad_in, gates, gw1, gb1, gw2, gb2, gow = outs
    return grad_in, gates, gw1, gb1[0], gw2, gb2[0], gow


def solution(mesh):
    def body(*arrays):
        rows, channels = arrays[0].shape
        count = mesh.shape["seq"]
        fits = channels == 128 * count and rows % 128 == 0 and count == 2 * SPAN
        if fits:
            return exchanged(mesh.shape, *arrays)
        return per_device(*arrays)

    in_specs = (
        P("seq", "ch"),
        P("seq", "ch"),
        P("seq", "ch"),
        P(),
        P(),
        P(),
        P(),
        P(None, "ch"),
        P("ch"),
        P("ch"),
    )
    out_specs = (P("seq", "ch"), P("seq", "ch"), P(), P(), P(), P(), P(None, "ch"))
    return jax.shard_map(
        body, mesh=mesh, in_specs=in_specs, out_specs=out_specs, check_vma=False
    )
```

```python
import math

import jax
import jax.numpy as jnp
import functools

import numpy as np
from jax import lax
from jax.experimental import pallas as pl
from jax.experimental.pallas import tpu as pltpu
from jax.sharding import PartitionSpec as P

SPAN = 4


FULL_PRECISION = lax.Precision.HIGHEST


def passed_along(value, axis, steps):
    count = lax.axis_size(axis)
    pairs = [(source, (source + steps) % count) for source in range(count)]
    return lax.ppermute(value, axis, pairs)


def angle_table(first_index, second_index, period):
    product = first_index[:, None] * second_index[None, :] % period
    return 2.0 * math.pi / period * product.astype(jnp.float32)


def lag_features(lag_count, feature_count):
    lag_index = jnp.arange(lag_count, dtype=jnp.int32)
    band_index = jnp.arange(feature_count // 2, dtype=jnp.int32) + 1
    phases = angle_table(lag_index, band_index, 2 * feature_count)
    return jnp.concatenate([jnp.cos(phases), jnp.sin(phases)], axis=1)


def split_table(table):
    upper_part = table.astype(jnp.bfloat16)
    lower_part = (table - upper_part.astype(jnp.float32)).astype(jnp.bfloat16)
    return (upper_part, lower_part)


def transform_tables(shard_rows):
    period = 2 * shard_rows
    frequency = jnp.arange(shard_rows + 1, dtype=jnp.int32)
    position = jnp.arange(shard_rows, dtype=jnp.int32)
    bin_weight = jnp.where((frequency == 0) | (frequency == shard_rows), 1.0, 2.0).astype(
        jnp.float32
    )
    forward_angles = angle_table(frequency, position, period)
    mirror_angles = angle_table(frequency, shard_rows - 1 - position, period)
    back_angles = angle_table(position + shard_rows, frequency, period)
    mirror_back = angle_table(2 * shard_rows - 1 - position, frequency, period)
    front_table = jnp.stack([jnp.cos(forward_angles), -jnp.sin(forward_angles)])
    mirror_table = jnp.stack([jnp.cos(mirror_angles), -jnp.sin(mirror_angles)])
    back_plain = jnp.stack([jnp.cos(back_angles), -jnp.sin(back_angles)]) / period
    back_table = back_plain * bin_weight[None, None, :]
    mirror_out = jnp.stack([jnp.cos(mirror_back), -jnp.sin(mirror_back)]) * (
        bin_weight[None, None, :] / period
    )
    fold_table = front_table * bin_weight[None, :, None]
    parity = (1.0 - 2.0 * (frequency % 2).astype(jnp.float32))[None, :, None]
    return (front_table, mirror_table, back_plain, back_table, mirror_out, fold_table, parity)


def spectrum(table_in, signal):
    return jnp.einsum("kfs,sc->kfc", table_in, signal, precision=FULL_PRECISION)


def sample_spectrum(table_pair, signal):
    upper_term = jnp.einsum(
        "kfs,sc->kfc", table_pair[0], signal, preferred_element_type=jnp.float32
    )
    lower_term = jnp.einsum(
        "kfs,sc->kfc", table_pair[1], signal, preferred_element_type=jnp.float32
    )
    return upper_term + lower_term


def sample_pullback(table_pair, signal):
    upper_term = jnp.einsum(
        "ksf,sc->kfc", table_pair[0], signal, preferred_element_type=jnp.float32
    )
    lower_term = jnp.einsum(
        "ksf,sc->kfc", table_pair[1], signal, preferred_element_type=jnp.float32
    )
    return upper_term + lower_term


def complex_product(left_factor, right_factor):
    real_part = left_factor[0] * right_factor[0] - left_factor[1] * right_factor[1]
    imag_part = left_factor[0] * right_factor[1] + left_factor[1] * right_factor[0]
    return jnp.stack([real_part, imag_part])


def conjugate_product(left_factor, right_factor):
    real_part = left_factor[0] * right_factor[0] + left_factor[1] * right_factor[1]
    imag_part = left_factor[1] * right_factor[0] - left_factor[0] * right_factor[1]
    return jnp.stack([real_part, imag_part])


def weighted_sum(filter_mixes, spectra_items):
    accumulated = complex_product(filter_mixes[0], spectra_items[0])
    for offset in range(1, len(filter_mixes)):
        accumulated = accumulated + complex_product(filter_mixes[offset], spectra_items[offset])
    return accumulated


def per_device(
    inputs,
    gate_values,
    grad_out,
    first_weight,
    first_bias,
    second_weight,
    second_bias,
    out_weight,
    decay_rates,
    mask_lengths,
):
    shard_rows = inputs.shape[0]
    window = SPAN * shard_rows
    front_table, mirror_table, back_plain, back_table, mirror_out, fold_table, parity = (
        transform_tables(shard_rows)
    )
    front_pair = split_table(front_table)
    mirror_pair = split_table(mirror_table)
    pull_pair = split_table(back_plain)
    features = lag_features(window, first_weight.shape[0])
    pre_first = jnp.dot(features, first_weight, precision=FULL_PRECISION) + first_bias
    hidden_one = jnp.sin(pre_first)
    pre_second = jnp.dot(hidden_one, second_weight, precision=FULL_PRECISION) + second_bias
    hidden_two = jnp.sin(pre_second)
    lag_index = jnp.arange(window, dtype=jnp.int32)
    envelope = jnp.exp(-decay_rates[None, :] * lag_index.astype(jnp.float32)[:, None]) * (
        lag_index[:, None] < mask_lengths[None, :]
    ).astype(jnp.float32)
    filter_taps = jnp.dot(hidden_two, out_weight, precision=FULL_PRECISION) * envelope
    block_spectra = [
        spectrum(front_table, filter_taps[block * shard_rows : (block + 1) * shard_rows])
        for block in range(SPAN)
    ]
    filter_mixes = []
    for offset in range(SPAN + 1):
        if offset == 0:
            mixed = parity * block_spectra[0]
        elif offset == SPAN:
            mixed = block_spectra[SPAN - 1]
        else:
            mixed = block_spectra[offset - 1] + parity * block_spectra[offset]
        filter_mixes.append(mixed)
    carried = (grad_out.astype(jnp.float32) * gate_values.astype(jnp.float32)).astype(jnp.bfloat16)
    earlier_spectra = [sample_spectrum(front_pair, inputs)]
    later_spectra = [sample_spectrum(mirror_pair, carried)]
    for offset in range(1, SPAN + 1):
        earlier = passed_along(inputs, "seq", offset)
        later = passed_along(carried, "seq", -offset)
        earlier_spectra.append(sample_spectrum(front_pair, earlier))
        later_spectra.append(sample_spectrum(mirror_pair, later))
    convolved = jnp.einsum(
        "ksf,kfc->sc",
        back_table,
        weighted_sum(filter_mixes, earlier_spectra),
        precision=FULL_PRECISION,
    )
    grad_gates = (grad_out.astype(jnp.float32) * convolved).astype(jnp.bfloat16)
    grad_inputs = jnp.einsum(
        "ksf,kfc->sc",
        mirror_out,
        weighted_sum(filter_mixes, later_spectra),
        precision=FULL_PRECISION,
    ).astype(jnp.bfloat16)
    pulled = sample_pullback(pull_pair, carried)
    grad_mixes = [conjugate_product(pulled, spectra_item) for spectra_item in earlier_spectra]
    pieces = []
    for block in range(SPAN):
        grad_block = parity * grad_mixes[block] + grad_mixes[block + 1]
        pieces.append(jnp.einsum("kfs,kfc->sc", fold_table, grad_block, precision=FULL_PRECISION))
    tap_terms = jnp.concatenate(pieces, axis=0)
    grad_scale = 1.0 / math.sqrt(lax.axis_size("seq") * shard_rows * window)
    tap_sums = lax.psum(tap_terms, "seq")
    grad_taps = tap_sums * envelope * grad_scale
    grad_out_weight = jnp.dot(hidden_two.T, grad_taps, precision=FULL_PRECISION)
    unit_grad = lax.psum(
        jnp.dot(grad_taps, out_weight.T, precision=FULL_PRECISION).astype(jnp.bfloat16), "ch"
    ).astype(jnp.float32)
    grad_two = unit_grad * jnp.cos(pre_second)
    grad_second_weight = jnp.dot(hidden_one.T, grad_two, precision=FULL_PRECISION)
    grad_second_bias = jnp.sum(grad_two, axis=0)
    grad_one = jnp.dot(grad_two, second_weight.T, precision=FULL_PRECISION) * jnp.cos(pre_first)
    grad_first_weight = jnp.dot(features.T, grad_one, precision=FULL_PRECISION)
    grad_first_bias = jnp.sum(grad_one, axis=0)
    return (
        grad_inputs,
        grad_gates,
        grad_first_weight,
        grad_first_bias,
        grad_second_weight,
        grad_second_bias,
        grad_out_weight,
    )


VMEM_LIMIT = 40_000_000
DRAIN_LIMIT = 8_000_000
EARLY, MIDDLE = 3, 5
MESH = pl.DeviceIdType.MESH


def bf(value):
    return value.astype(jnp.bfloat16)


def dot(left, right, dims=((1,), (0,)), precision=None):
    return lax.dot_general(
        left, right, (dims, ((), ())), precision=precision, preferred_element_type=jnp.float32
    )


def packed_table(tokens):
    half = tokens // 2
    freq = np.arange(half)[:, None]
    time = np.arange(tokens)[None, :]
    angles = 2.0 * np.pi / tokens * (freq * time % tokens)
    lower = -np.sin(angles)
    lower[0] = 1.0 - 2.0 * (np.arange(tokens) % 2)
    return np.concatenate([np.cos(angles), lower]).astype(np.float32)


def exchange_kernel(
    sizes, x_hbm, gate_hbm, gout_hbm, w1_hbm, b1_hbm, w2_hbm, b2_hbm, decay_hbm, mask_hbm,
    feat_hbm, featt_hbm, ow_hbm, table_hbm, turned_hbm,
    gi_ref, gg_ref, gw1_ref, gb1_ref, gw2_ref, gb2_ref, gow_ref,
    gate_ref, gout_ref, w1_ref, b1_ref, w2_ref, b2_ref, decay_ref, mask_ref,
    feat_ref, featt_ref, ow, table, turned,
    ow_turned, ow_rest, carried, xs, cs, conv_in, taps, env, xspec, cspec, tspec, prod_v, prod_t,
    prod_g, back_v, back_g, sums, gts, gtall, units, send_sem, recv_sem, usend, urecv,
    local_sem, late_sem,
):
    n, m, rows, width, window, period = sizes
    tokens = n * rows
    half = tokens // 2
    side = n // 2
    me = lax.axis_index("seq")
    mine = lax.axis_index("ch")
    early = n // 4
    late = n - early
    steps = range(1, n)
    others = {step: lax.rem(mine + step, m) for step in range(1, m)}
    last = me >= late
    base_peer = me // side * side
    near = [base_peer + lax.rem(me - base_peer + step, side) for step in range(1, side)]
    across = lax.rem(me + side, n)
    far = [side - base_peer + lax.rem(me - base_peer + step, side) for step in range(side)]

    barrier = pltpu.get_barrier_semaphore()

    def greet(peer):
        pl.semaphore_signal(barrier, inc=1, device_id={"seq": peer}, device_id_type=MESH)

    for at in range(late, n):
        @pl.when(me != at)
        def _():
            greet(at)

    @pl.when(jnp.logical_not(last))
    def _():
        for step in range(1, late):
            greet(lax.rem(me + step, late))

    for step in range(1, m):
        pl.semaphore_signal(barrier, inc=1, device_id={"ch": others[step]}, device_id_type=MESH)

    own_rows = pl.ds(pl.multiple_of(me * rows, rows), rows)
    own_cols = pl.ds(pl.multiple_of(me * width, width), width)
    loads = []
    for at, (source, target) in enumerate((
        (gate_hbm, gate_ref), (gout_hbm, gout_ref), (x_hbm.at[:, own_cols], xs.at[own_rows, :]),
        (w1_hbm, w1_ref), (b1_hbm, b1_ref), (w2_hbm, w2_ref), (b2_hbm, b2_ref),
        (decay_hbm, decay_ref), (mask_hbm, mask_ref), (feat_hbm, feat_ref),
        (featt_hbm, featt_ref), (ow_hbm, ow), (table_hbm, table), (turned_hbm, turned),
    )):
        load = pltpu.make_async_copy(source, target, local_sem.at[at])
        load.start()
        loads.append(load)
    pl.semaphore_wait(barrier, jnp.where(last, n - 1, late - 1) + m - 1)

    @pl.when(last)
    def _():
        for at in range(late):
            pl.semaphore_signal(late_sem, inc=1, device_id={"seq": at}, device_id_type=MESH)

    def move(kind, step, source, target):
        return pltpu.make_async_remote_copy(
            src_ref=source, dst_ref=target,
            send_sem=send_sem.at[kind, step], recv_sem=recv_sem.at[kind, step],
            device_id={"seq": lax.rem(me + step, n)}, device_id_type=MESH,
        )

    def ahead(peer):
        return lax.rem(peer - me + n, n)

    def columns(peer):
        return pl.ds(pl.multiple_of(peer * width, width), width)

    def block(peer):
        return pl.ds(pl.multiple_of(peer * rows, rows), rows)

    x_moves = [move(0, step, xs.at[own_rows, :], xs.at[own_rows, :]) for step in steps]
    c_moves = [move(1, step, cs.at[own_rows, :], cs.at[own_rows, :]) for step in steps]
    for at in range(n - 1):
        around = lax.rem(me + 1 + at, n)
        ahead_of = lax.rem(me + 1 + at, late) if at < late - 1 else at + 1
        peer = jnp.where(last, around, ahead_of)
        if at == late - 1:

            @pl.when(jnp.logical_not(last))
            def _():
                pl.semaphore_wait(late_sem, n - late)

        move(0, ahead(peer), x_hbm.at[:, columns(peer)], xs.at[own_rows, :]).start()
    for load in loads[:2]:
        load.wait()
    carried[...] = bf(gout_ref[...].astype(jnp.float32) * gate_ref[...].astype(jnp.float32))
    for at in range(n - 1):
        around = lax.rem(me + 1 + at, n)
        ahead_of = lax.rem(me + 1 + at, late) if at < late - 1 else at + 1
        peer = jnp.where(last, around, ahead_of)
        move(1, ahead(peer), carried.at[:, columns(peer)], cs.at[own_rows, :]).start()
    cs[own_rows, :] = carried[:, own_cols]

    full = lax.Precision.HIGHEST
    for load in loads[2:]:
        load.wait()
    pre_one = dot(feat_ref[...], w1_ref[...], precision=full) + b1_ref[...]
    h_one = jnp.sin(pre_one)
    slope_one = jnp.cos(pre_one)
    pre_two = dot(h_one, w2_ref[...], precision=full) + b2_ref[...]
    h_two = jnp.sin(pre_two)
    slope_two = jnp.cos(pre_two)
    base = dot(h_two, ow[:, own_cols], precision=full)
    decay = decay_ref[:, own_cols]
    lengths = mask_ref[:, own_cols]
    for at in range(window // period):
        lag = lax.broadcasted_iota(jnp.int32, (period, width), 0) + at * period
        part = jnp.where(lag < lengths, jnp.exp(-decay * lag.astype(jnp.float32)), 0.0)
        env[pl.ds(at * period, period), :] = part
        taps[pl.ds(at * period, period), :] = bf(base * part)

    tspec[...] = dot(table[:, 0:window], taps[...])

    h_one_t = bf(h_one.T)
    w2_whole = w2_ref[...].T
    w2_turned = bf(w2_whole)
    w2_rest = bf(w2_whole - w2_turned.astype(jnp.float32))
    turned_ow = ow[...].T
    ow_turned[...] = bf(turned_ow)
    ow_rest[...] = bf(turned_ow - bf(turned_ow).astype(jnp.float32))
    h_two_t = bf(h_two.T)

    def parts(i):
        upper = pl.ds(pl.multiple_of(i * 64, 64), 64)
        lower = pl.ds(pl.multiple_of(half + i * 64, 64), 64)
        first = (lax.broadcasted_iota(jnp.int32, (64, width), 0) + i * 64) == 0
        weight = jnp.where(first, 1.0 / tokens, 2.0 / tokens)
        return upper, lower, first, weight

    for copy in x_moves:
        copy.wait_recv()

    xspec[...] = dot(table[...], xs[...])

    @pl.loop(0, half // 64)
    def _(i):
        upper, lower, first, weight = parts(i)
        xr, xi = xspec[upper, :], xspec[lower, :]
        hr, hi = tspec[upper, :], tspec[lower, :]
        hx = hi * xi
        prod_v[upper, :] = bf((hr * xr - jnp.where(first, 0.0, hx)) * weight)
        prod_v[lower, :] = bf(jnp.where(first, hx, hr * xi + hi * xr) * weight)

    back_v[...] = bf(dot(turned[...], prod_v[...]))

    v_moves = [
        move(2, step, back_v.at[own_rows, :], conv_in.at[:, own_cols]) for step in steps
    ]

    def send_conv(some):
        for step in some:
            peer = lax.rem(me + step, n)
            move(2, step, back_v.at[block(peer), :], conv_in.at[:, own_cols]).start()

    send_conv(steps[:EARLY])
    conv_in[:, own_cols] = back_v[own_rows, :]

    def arrived(kind, peer, target):
        move(kind, lax.rem(me - peer + n, n), target, target).wait_recv()

    near_span = pl.ds(pl.multiple_of(base_peer * rows, half), half)
    far_span = pl.ds(pl.multiple_of((side - base_peer) * rows, half), half)
    for peer in near:
        arrived(1, peer, cs.at[own_rows, :])
    cspec[...] = dot(table[:, near_span], cs[near_span, :])
    for peer in far:
        arrived(1, peer, cs.at[own_rows, :])
    cspec[...] += dot(table[:, far_span], cs[far_span, :])

    @pl.loop(0, half // 64)
    def _(i):
        upper, lower, first, weight = parts(i)
        xr, xi = xspec[upper, :], xspec[lower, :]
        cr, ci = cspec[upper, :], cspec[lower, :]
        cx = ci * xi
        prod_t[upper, :] = bf((cr * xr + jnp.where(first, 0.0, cx)) * weight)
        prod_t[lower, :] = bf(jnp.where(first, cx, ci * xr - cr * xi) * weight)

    sums[...] = dot(turned[0:window, :], prod_t[...])

    folded = sums[0:period, :] * env[0:period, :]
    for at in range(1, window // period):
        piece = pl.ds(at * period, period)
        folded = folded + sums[piece, :] * env[piece, :]
    folded = bf(folded * (1.0 / math.sqrt(tokens * window)))
    gts[...] = folded
    gtall[:, own_cols] = folded

    def give(peer):
        return move(4, ahead(peer), gts, gtall.at[:, own_cols])

    def taken(kind, peer):
        return move(kind, lax.rem(me - peer + n, n), gts, gtall.at[:, own_cols])

    give(across).start()
    for at in range(early):
        @pl.when((me >= side) & (across != at))
        def _():
            give(at).start()


    for peer in near:
        give(peer).start()
    send_conv(steps[EARLY:MIDDLE])

    @pl.loop(0, half // 64)
    def _(i):
        upper, lower, first, weight = parts(i)
        cr, ci = cspec[upper, :], cspec[lower, :]
        hr, hi = tspec[upper, :], tspec[lower, :]
        hc = hi * ci
        prod_g[upper, :] = bf((hr * cr + jnp.where(first, 0.0, hc)) * weight)
        prod_g[lower, :] = bf(jnp.where(first, hc, hr * ci - hi * cr) * weight)

    back_g[...] = bf(dot(turned[...], prod_g[...]))


    def forward(peer):
        return move(5, ahead(peer), gtall.at[:, columns(across)], gtall.at[:, columns(across)])

    def give_back(some):
        for at in some:
            rising = at + (me <= at).astype(jnp.int32)
            peer = jnp.where(lax.rem(mine, 2) == 0, rising, lax.rem(me + 1 + at, n))
            move(3, ahead(peer), back_g.at[block(peer), :], gi_ref.at[:, own_cols]).start()

    lower = me < side

    @pl.when(lower)
    def _():
        give_back(range(1))

    taken(4, across).wait_recv()

    @pl.when(me >= side)
    def _():
        for peer in near:
            forward(peer).start()

    for at in range(early, side):
        @pl.when((me < side) & (me != at))
        def _():
            forward(at).start()


    g_moves = [move(3, step, back_g.at[own_rows, :], gi_ref.at[:, own_cols]) for step in steps]
    @pl.when(jnp.logical_not(lower))
    def _():
        give_back(range(1))

    give_back(range(1, n - 1))
    send_conv(steps[MIDDLE:])
    gi_ref[:, own_cols] = back_g[own_rows, :]
    for peer in near:
        taken(4, peer).wait_recv()

    def unit_part(first):
        span = pl.ds(pl.multiple_of(first * width, side * width), side * width)
        return dot(gtall[:, span], ow_turned[span, :]) + dot(gtall[:, span], ow_rest[span, :])

    near_part = unit_part(base_peer)

    @pl.when(me >= side)
    def _():
        for peer in near:
            taken(5, peer).wait_recv()

    @pl.when(me < early)
    def _():
        for peer in far[1:]:
            taken(4, peer).wait_recv()

    @pl.when((me >= early) & (me < side))
    def _():
        for at in range(early):
            taken(5, at).wait_recv()
        for step in range(1, side - early):
            taken(5, early + lax.rem(me - early + step, side - early)).wait_recv()


    units[mine] = bf(near_part + unit_part(side - base_peer))
    crossing = []
    for step in range(1, m):
        copy = pltpu.make_async_remote_copy(
            src_ref=units.at[mine], dst_ref=units.at[mine],
            send_sem=usend.at[step], recv_sem=urecv.at[step],
            device_id={"ch": others[step]}, device_id_type=MESH,
        )
        copy.start()
        crossing.append(copy)
    gow_ref[...] = dot(h_two_t, gtall[...])
    for copy in v_moves:
        copy.wait_recv()
    gg_ref[...] = bf(gout_ref[...].astype(jnp.float32) * conv_in[...].astype(jnp.float32))
    for copy in crossing:
        copy.wait_recv()
    unit = units[0].astype(jnp.float32)
    for other in range(1, m):
        unit = unit + units[other].astype(jnp.float32)
    grad_two = unit * slope_two
    narrow_two = bf(grad_two)
    grad_one = (dot(narrow_two, w2_turned) + dot(narrow_two, w2_rest)) * slope_one
    gw1_ref[...] = dot(featt_ref[...], grad_one, precision=full)
    gw2_ref[...] = dot(h_one_t, narrow_two)
    gb2_ref[...] = jnp.sum(grad_two, axis=0, keepdims=True)
    gb1_ref[...] = jnp.sum(grad_one, axis=0, keepdims=True)
    for copy in x_moves + c_moves + v_moves:
        copy.wait_send()
    for peer in near:
        give(peer).wait_send()

    give(across).wait_send()
    for at in range(early):
        @pl.when((me >= side) & (across != at))
        def _():
            give(at).wait_send()

    @pl.when(me >= side)
    def _():
        for peer in near:
            forward(peer).wait_send()

    for at in range(early, side):
        @pl.when((me < side) & (me != at))
        def _():
            forward(at).wait_send()

    for copy in crossing:
        copy.wait_send()
    for copy in g_moves:
        copy.wait()


def drain_kernel(*refs):
    count = len(refs) // 2
    store_sem = refs[-1]
    stores = [
        pltpu.make_async_copy(refs[at], refs[count + at], store_sem.at[at])
        for at in range(count)
    ]
    for copy in stores:
        copy.start()
    for copy in stores:
        copy.wait()


def exchanged(
    mesh_shape, inputs, gate_values, grad_out, first_weight, first_bias, second_weight,
    second_bias, out_weight, decay_rates, mask_lengths,
):
    n, m = mesh_shape["seq"], mesh_shape["ch"]
    rows, channels = inputs.shape
    width = channels // n
    window = SPAN * rows
    emb, units = first_weight.shape
    period = 2 * emb
    tokens = n * rows
    angles = (
        2.0 * np.pi / period
        * (np.arange(period)[:, None] * (np.arange(emb // 2)[None, :] + 1) % period)
    )
    features = np.concatenate([np.cos(angles), np.sin(angles)], axis=1).astype(np.float32)
    f32, b16 = jnp.float32, jnp.bfloat16
    outside = pl.BlockSpec(memory_space=pltpu.HBM)
    inside = pl.BlockSpec(memory_space=pltpu.VMEM)
    shape = jax.ShapeDtypeStruct
    sem = pltpu.SemaphoreType.DMA
    table = packed_table(tokens)
    staged = (
        gate_values, grad_out, first_weight, first_bias[None], second_weight,
        second_bias[None], decay_rates[None], mask_lengths[None],
        jnp.asarray(features), jnp.asarray(features.T.copy()), out_weight,
        jnp.asarray(table, dtype=b16), jnp.asarray(table.T.copy(), dtype=b16),
    )
    out_shapes = (
        shape((rows, channels), b16), shape((rows, channels), b16),
        shape((emb, units), f32), shape((1, units), f32),
        shape((units, units), f32), shape((1, units), f32),
        shape((units, channels), f32),
    )
    outs = pl.pallas_call(
        functools.partial(exchange_kernel, (n, m, rows, width, window, period)),
        out_shape=tuple(pltpu.VMEM(out.shape, out.dtype) for out in out_shapes),
        in_specs=[outside] * 14,
        out_specs=(inside,) * 7,
        scratch_shapes=[
            *[pltpu.VMEM(array.shape, array.dtype) for array in staged],
            pltpu.VMEM((channels, units), b16), pltpu.VMEM((channels, units), b16),
            pltpu.VMEM((rows, channels), b16),
            pltpu.VMEM((tokens, width), b16), pltpu.VMEM((tokens, width), b16),
            pltpu.VMEM((rows, channels), b16),
            pltpu.VMEM((window, width), b16), pltpu.VMEM((window, width), f32),
            pltpu.VMEM((tokens, width), f32), pltpu.VMEM((tokens, width), f32),
            pltpu.VMEM((tokens, width), f32),
            pltpu.VMEM((tokens, width), b16), pltpu.VMEM((tokens, width), b16),
            pltpu.VMEM((tokens, width), b16),
            pltpu.VMEM((tokens, width), b16), pltpu.VMEM((tokens, width), b16),
            pltpu.VMEM((window, width), f32),
            pltpu.VMEM((period, width), b16), pltpu.VMEM((period, channels), b16),
            pltpu.VMEM((m, period, units), b16),
            sem((6, n)), sem((6, n)), sem((m,)), sem((m,)), sem((14,)),
            pltpu.SemaphoreType.REGULAR,
        ],
        compiler_params=pltpu.CompilerParams(
            collective_id=0, has_side_effects=True, vmem_limit_bytes=VMEM_LIMIT
        ),
        name="exchange",
    )(*[pltpu.with_memory_space_constraint(array, pltpu.HBM) for array in (inputs, *staged)])
    outs = pl.pallas_call(
        drain_kernel,
        out_shape=out_shapes,
        in_specs=[inside] * 7,
        out_specs=(outside,) * 7,
        scratch_shapes=[sem((7,))],
        compiler_params=pltpu.CompilerParams(vmem_limit_bytes=DRAIN_LIMIT),
        name="drain",
    )(*outs)
    grad_in, gates, gw1, gb1, gw2, gb2, gow = outs
    return grad_in, gates, gw1, gb1[0], gw2, gb2[0], gow


def solution(mesh):
    def body(*arrays):
        rows, channels = arrays[0].shape
        count = mesh.shape["seq"]
        fits = channels == 128 * count and rows % 128 == 0 and count == 2 * SPAN
        if fits:
            return exchanged(mesh.shape, *arrays)
        return per_device(*arrays)

    in_specs = (
        P("seq", "ch"),
        P("seq", "ch"),
        P("seq", "ch"),
        P(),
        P(),
        P(),
        P(),
        P(None, "ch"),
        P("ch"),
        P("ch"),
    )
    out_specs = (P("seq", "ch"), P("seq", "ch"), P(), P(), P(), P(), P(None, "ch"))
    return jax.shard_map(
        body, mesh=mesh, in_specs=in_specs, out_specs=out_specs, check_vma=False
    )
```

```python
import math

import jax
import jax.numpy as jnp
import functools

import numpy as np
from jax import lax
from jax.experimental import pallas as pl
from jax.experimental.pallas import tpu as pltpu
from jax.sharding import PartitionSpec as P

SPAN = 4


FULL_PRECISION = lax.Precision.HIGHEST


def passed_along(value, axis, steps):
    count = lax.axis_size(axis)
    pairs = [(source, (source + steps) % count) for source in range(count)]
    return lax.ppermute(value, axis, pairs)


def angle_table(first_index, second_index, period):
    product = first_index[:, None] * second_index[None, :] % period
    return 2.0 * math.pi / period * product.astype(jnp.float32)


def lag_features(lag_count, feature_count):
    lag_index = jnp.arange(lag_count, dtype=jnp.int32)
    band_index = jnp.arange(feature_count // 2, dtype=jnp.int32) + 1
    phases = angle_table(lag_index, band_index, 2 * feature_count)
    return jnp.concatenate([jnp.cos(phases), jnp.sin(phases)], axis=1)


def split_table(table):
    upper_part = table.astype(jnp.bfloat16)
    lower_part = (table - upper_part.astype(jnp.float32)).astype(jnp.bfloat16)
    return (upper_part, lower_part)


def transform_tables(shard_rows):
    period = 2 * shard_rows
    frequency = jnp.arange(shard_rows + 1, dtype=jnp.int32)
    position = jnp.arange(shard_rows, dtype=jnp.int32)
    bin_weight = jnp.where((frequency == 0) | (frequency == shard_rows), 1.0, 2.0).astype(
        jnp.float32
    )
    forward_angles = angle_table(frequency, position, period)
    mirror_angles = angle_table(frequency, shard_rows - 1 - position, period)
    back_angles = angle_table(position + shard_rows, frequency, period)
    mirror_back = angle_table(2 * shard_rows - 1 - position, frequency, period)
    front_table = jnp.stack([jnp.cos(forward_angles), -jnp.sin(forward_angles)])
    mirror_table = jnp.stack([jnp.cos(mirror_angles), -jnp.sin(mirror_angles)])
    back_plain = jnp.stack([jnp.cos(back_angles), -jnp.sin(back_angles)]) / period
    back_table = back_plain * bin_weight[None, None, :]
    mirror_out = jnp.stack([jnp.cos(mirror_back), -jnp.sin(mirror_back)]) * (
        bin_weight[None, None, :] / period
    )
    fold_table = front_table * bin_weight[None, :, None]
    parity = (1.0 - 2.0 * (frequency % 2).astype(jnp.float32))[None, :, None]
    return (front_table, mirror_table, back_plain, back_table, mirror_out, fold_table, parity)


def spectrum(table_in, signal):
    return jnp.einsum("kfs,sc->kfc", table_in, signal, precision=FULL_PRECISION)


def sample_spectrum(table_pair, signal):
    upper_term = jnp.einsum(
        "kfs,sc->kfc", table_pair[0], signal, preferred_element_type=jnp.float32
    )
    lower_term = jnp.einsum(
        "kfs,sc->kfc", table_pair[1], signal, preferred_element_type=jnp.float32
    )
    return upper_term + lower_term


def sample_pullback(table_pair, signal):
    upper_term = jnp.einsum(
        "ksf,sc->kfc", table_pair[0], signal, preferred_element_type=jnp.float32
    )
    lower_term = jnp.einsum(
        "ksf,sc->kfc", table_pair[1], signal, preferred_element_type=jnp.float32
    )
    return upper_term + lower_term


def complex_product(left_factor, right_factor):
    real_part = left_factor[0] * right_factor[0] - left_factor[1] * right_factor[1]
    imag_part = left_factor[0] * right_factor[1] + left_factor[1] * right_factor[0]
    return jnp.stack([real_part, imag_part])


def conjugate_product(left_factor, right_factor):
    real_part = left_factor[0] * right_factor[0] + left_factor[1] * right_factor[1]
    imag_part = left_factor[1] * right_factor[0] - left_factor[0] * right_factor[1]
    return jnp.stack([real_part, imag_part])


def weighted_sum(filter_mixes, spectra_items):
    accumulated = complex_product(filter_mixes[0], spectra_items[0])
    for offset in range(1, len(filter_mixes)):
        accumulated = accumulated + complex_product(filter_mixes[offset], spectra_items[offset])
    return accumulated


def per_device(
    inputs,
    gate_values,
    grad_out,
    first_weight,
    first_bias,
    second_weight,
    second_bias,
    out_weight,
    decay_rates,
    mask_lengths,
):
    shard_rows = inputs.shape[0]
    window = SPAN * shard_rows
    front_table, mirror_table, back_plain, back_table, mirror_out, fold_table, parity = (
        transform_tables(shard_rows)
    )
    front_pair = split_table(front_table)
    mirror_pair = split_table(mirror_table)
    pull_pair = split_table(back_plain)
    features = lag_features(window, first_weight.shape[0])
    pre_first = jnp.dot(features, first_weight, precision=FULL_PRECISION) + first_bias
    hidden_one = jnp.sin(pre_first)
    pre_second = jnp.dot(hidden_one, second_weight, precision=FULL_PRECISION) + second_bias
    hidden_two = jnp.sin(pre_second)
    lag_index = jnp.arange(window, dtype=jnp.int32)
    envelope = jnp.exp(-decay_rates[None, :] * lag_index.astype(jnp.float32)[:, None]) * (
        lag_index[:, None] < mask_lengths[None, :]
    ).astype(jnp.float32)
    filter_taps = jnp.dot(hidden_two, out_weight, precision=FULL_PRECISION) * envelope
    block_spectra = [
        spectrum(front_table, filter_taps[block * shard_rows : (block + 1) * shard_rows])
        for block in range(SPAN)
    ]
    filter_mixes = []
    for offset in range(SPAN + 1):
        if offset == 0:
            mixed = parity * block_spectra[0]
        elif offset == SPAN:
            mixed = block_spectra[SPAN - 1]
        else:
            mixed = block_spectra[offset - 1] + parity * block_spectra[offset]
        filter_mixes.append(mixed)
    carried = (grad_out.astype(jnp.float32) * gate_values.astype(jnp.float32)).astype(jnp.bfloat16)
    earlier_spectra = [sample_spectrum(front_pair, inputs)]
    later_spectra = [sample_spectrum(mirror_pair, carried)]
    for offset in range(1, SPAN + 1):
        earlier = passed_along(inputs, "seq", offset)
        later = passed_along(carried, "seq", -offset)
        earlier_spectra.append(sample_spectrum(front_pair, earlier))
        later_spectra.append(sample_spectrum(mirror_pair, later))
    convolved = jnp.einsum(
        "ksf,kfc->sc",
        back_table,
        weighted_sum(filter_mixes, earlier_spectra),
        precision=FULL_PRECISION,
    )
    grad_gates = (grad_out.astype(jnp.float32) * convolved).astype(jnp.bfloat16)
    grad_inputs = jnp.einsum(
        "ksf,kfc->sc",
        mirror_out,
        weighted_sum(filter_mixes, later_spectra),
        precision=FULL_PRECISION,
    ).astype(jnp.bfloat16)
    pulled = sample_pullback(pull_pair, carried)
    grad_mixes = [conjugate_product(pulled, spectra_item) for spectra_item in earlier_spectra]
    pieces = []
    for block in range(SPAN):
        grad_block = parity * grad_mixes[block] + grad_mixes[block + 1]
        pieces.append(jnp.einsum("kfs,kfc->sc", fold_table, grad_block, precision=FULL_PRECISION))
    tap_terms = jnp.concatenate(pieces, axis=0)
    grad_scale = 1.0 / math.sqrt(lax.axis_size("seq") * shard_rows * window)
    tap_sums = lax.psum(tap_terms, "seq")
    grad_taps = tap_sums * envelope * grad_scale
    grad_out_weight = jnp.dot(hidden_two.T, grad_taps, precision=FULL_PRECISION)
    unit_grad = lax.psum(
        jnp.dot(grad_taps, out_weight.T, precision=FULL_PRECISION).astype(jnp.bfloat16), "ch"
    ).astype(jnp.float32)
    grad_two = unit_grad * jnp.cos(pre_second)
    grad_second_weight = jnp.dot(hidden_one.T, grad_two, precision=FULL_PRECISION)
    grad_second_bias = jnp.sum(grad_two, axis=0)
    grad_one = jnp.dot(grad_two, second_weight.T, precision=FULL_PRECISION) * jnp.cos(pre_first)
    grad_first_weight = jnp.dot(features.T, grad_one, precision=FULL_PRECISION)
    grad_first_bias = jnp.sum(grad_one, axis=0)
    return (
        grad_inputs,
        grad_gates,
        grad_first_weight,
        grad_first_bias,
        grad_second_weight,
        grad_second_bias,
        grad_out_weight,
    )


VMEM_LIMIT = 40_000_000
DRAIN_LIMIT = 8_000_000
EARLY, MIDDLE = 3, 5
MESH = pl.DeviceIdType.MESH


def bf(value):
    return value.astype(jnp.bfloat16)


def dot(left, right, dims=((1,), (0,)), precision=None):
    return lax.dot_general(
        left, right, (dims, ((), ())), precision=precision, preferred_element_type=jnp.float32
    )


def packed_table(tokens):
    half = tokens // 2
    freq = np.arange(half)[:, None]
    time = np.arange(tokens)[None, :]
    angles = 2.0 * np.pi / tokens * (freq * time % tokens)
    lower = -np.sin(angles)
    lower[0] = 1.0 - 2.0 * (np.arange(tokens) % 2)
    return np.concatenate([np.cos(angles), lower]).astype(np.float32)


def exchange_kernel(
    sizes, x_hbm, gate_hbm, gout_hbm, w1_hbm, b1_hbm, w2_hbm, b2_hbm, decay_hbm, mask_hbm,
    feat_hbm, featt_hbm, ow_hbm, table_hbm, turned_hbm,
    gi_ref, gg_ref, gw1_ref, gb1_ref, gw2_ref, gb2_ref, gow_ref,
    gate_ref, gout_ref, w1_ref, b1_ref, w2_ref, b2_ref, decay_ref, mask_ref,
    feat_ref, featt_ref, ow, table, turned,
    ow_turned, ow_rest, carried, xs, cs, conv_in, taps, env, xspec, cspec, tspec, prod_v, prod_t,
    prod_g, back_v, back_g, sums, gts, gtall, units, send_sem, recv_sem, usend, urecv,
    local_sem, late_sem,
):
    n, m, rows, width, window, period = sizes
    tokens = n * rows
    half = tokens // 2
    side = n // 2
    me = lax.axis_index("seq")
    mine = lax.axis_index("ch")
    early = n // 4
    late = n - early
    steps = range(1, n)
    others = {step: lax.rem(mine + step, m) for step in range(1, m)}
    last = me >= late
    base_peer = me // side * side
    near = [base_peer + lax.rem(me - base_peer + step, side) for step in range(1, side)]
    across = lax.rem(me + side, n)
    far = [side - base_peer + lax.rem(me - base_peer + step, side) for step in range(side)]

    barrier = pltpu.get_barrier_semaphore()

    def greet(peer):
        pl.semaphore_signal(barrier, inc=1, device_id={"seq": peer}, device_id_type=MESH)

    for at in range(late, n):
        @pl.when(me != at)
        def _():
            greet(at)

    @pl.when(jnp.logical_not(last))
    def _():
        for step in range(1, late):
            greet(lax.rem(me + step, late))

    for step in range(1, m):
        pl.semaphore_signal(barrier, inc=1, device_id={"ch": others[step]}, device_id_type=MESH)

    own_rows = pl.ds(pl.multiple_of(me * rows, rows), rows)
    own_cols = pl.ds(pl.multiple_of(me * width, width), width)
    loads = []
    for at, (source, target) in enumerate((
        (gate_hbm, gate_ref), (gout_hbm, gout_ref), (x_hbm.at[:, own_cols], xs.at[own_rows, :]),
        (w1_hbm, w1_ref), (b1_hbm, b1_ref), (w2_hbm, w2_ref), (b2_hbm, b2_ref),
        (decay_hbm, decay_ref), (mask_hbm, mask_ref), (feat_hbm, feat_ref),
        (featt_hbm, featt_ref), (ow_hbm, ow), (table_hbm, table), (turned_hbm, turned),
    )):
        load = pltpu.make_async_copy(source, target, local_sem.at[at])
        load.start()
        loads.append(load)
    pl.semaphore_wait(barrier, jnp.where(last, n - 1, late - 1) + m - 1)

    @pl.when(last)
    def _():
        for at in range(late):
            pl.semaphore_signal(late_sem, inc=1, device_id={"seq": at}, device_id_type=MESH)

    def move(kind, step, source, target):
        return pltpu.make_async_remote_copy(
            src_ref=source, dst_ref=target,
            send_sem=send_sem.at[kind, step], recv_sem=recv_sem.at[kind, step],
            device_id={"seq": lax.rem(me + step, n)}, device_id_type=MESH,
        )

    def ahead(peer):
        return lax.rem(peer - me + n, n)

    def columns(peer):
        return pl.ds(pl.multiple_of(peer * width, width), width)

    def block(peer):
        return pl.ds(pl.multiple_of(peer * rows, rows), rows)

    x_moves = [move(0, step, xs.at[own_rows, :], xs.at[own_rows, :]) for step in steps]
    c_moves = [move(1, step, cs.at[own_rows, :], cs.at[own_rows, :]) for step in steps]
    for at in range(n - 1):
        around = lax.rem(me + 1 + at, n)
        ahead_of = lax.rem(me + late - 1 - at, late) if at < late - 1 else at + 1
        peer = jnp.where(last, around, ahead_of)
        if at == late - 1:

            @pl.when(jnp.logical_not(last))
            def _():
                pl.semaphore_wait(late_sem, n - late)

        move(0, ahead(peer), x_hbm.at[:, columns(peer)], xs.at[own_rows, :]).start()
    for load in loads[:2]:
        load.wait()
    carried[...] = bf(gout_ref[...].astype(jnp.float32) * gate_ref[...].astype(jnp.float32))
    for at in range(n - 1):
        around = lax.rem(me + 1 + at, n)
        ahead_of = lax.rem(me + 1 + at, late) if at < late - 1 else at + 1
        peer = jnp.where(last, around, ahead_of)
        move(1, ahead(peer), carried.at[:, columns(peer)], cs.at[own_rows, :]).start()
    cs[own_rows, :] = carried[:, own_cols]

    full = lax.Precision.HIGHEST
    for load in loads[2:]:
        load.wait()
    pre_one = dot(feat_ref[...], w1_ref[...], precision=full) + b1_ref[...]
    h_one = jnp.sin(pre_one)
    slope_one = jnp.cos(pre_one)
    pre_two = dot(h_one, w2_ref[...], precision=full) + b2_ref[...]
    h_two = jnp.sin(pre_two)
    slope_two = jnp.cos(pre_two)
    base = dot(h_two, ow[:, own_cols], precision=full)
    decay = decay_ref[:, own_cols]
    lengths = mask_ref[:, own_cols]
    for at in range(window // period):
        lag = lax.broadcasted_iota(jnp.int32, (period, width), 0) + at * period
        part = jnp.where(lag < lengths, jnp.exp(-decay * lag.astype(jnp.float32)), 0.0)
        env[pl.ds(at * period, period), :] = part
        taps[pl.ds(at * period, period), :] = bf(base * part)

    tspec[...] = dot(table[:, 0:window], taps[...])

    h_one_t = bf(h_one.T)
    w2_whole = w2_ref[...].T
    w2_turned = bf(w2_whole)
    w2_rest = bf(w2_whole - w2_turned.astype(jnp.float32))
    turned_ow = ow[...].T
    ow_turned[...] = bf(turned_ow)
    ow_rest[...] = bf(turned_ow - bf(turned_ow).astype(jnp.float32))
    h_two_t = bf(h_two.T)

    def parts(i):
        upper = pl.ds(pl.multiple_of(i * 64, 64), 64)
        lower = pl.ds(pl.multiple_of(half + i * 64, 64), 64)
        first = (lax.broadcasted_iota(jnp.int32, (64, width), 0) + i * 64) == 0
        weight = jnp.where(first, 1.0 / tokens, 2.0 / tokens)
        return upper, lower, first, weight

    for copy in x_moves:
        copy.wait_recv()

    xspec[...] = dot(table[...], xs[...])

    @pl.loop(0, half // 64)
    def _(i):
        upper, lower, first, weight = parts(i)
        xr, xi = xspec[upper, :], xspec[lower, :]
        hr, hi = tspec[upper, :], tspec[lower, :]
        hx = hi * xi
        prod_v[upper, :] = bf((hr * xr - jnp.where(first, 0.0, hx)) * weight)
        prod_v[lower, :] = bf(jnp.where(first, hx, hr * xi + hi * xr) * weight)

    back_v[...] = bf(dot(turned[...], prod_v[...]))

    v_moves = [
        move(2, step, back_v.at[own_rows, :], conv_in.at[:, own_cols]) for step in steps
    ]

    def send_conv(some):
        for step in some:
            peer = lax.rem(me + step, n)
            move(2, step, back_v.at[block(peer), :], conv_in.at[:, own_cols]).start()

    send_conv(steps[:EARLY])
    conv_in[:, own_cols] = back_v[own_rows, :]

    def arrived(kind, peer, target):
        move(kind, lax.rem(me - peer + n, n), target, target).wait_recv()

    near_span = pl.ds(pl.multiple_of(base_peer * rows, half), half)
    far_span = pl.ds(pl.multiple_of((side - base_peer) * rows, half), half)
    for peer in near:
        arrived(1, peer, cs.at[own_rows, :])
    cspec[...] = dot(table[:, near_span], cs[near_span, :])
    for peer in far:
        arrived(1, peer, cs.at[own_rows, :])
    cspec[...] += dot(table[:, far_span], cs[far_span, :])

    @pl.loop(0, half // 64)
    def _(i):
        upper, lower, first, weight = parts(i)
        xr, xi = xspec[upper, :], xspec[lower, :]
        cr, ci = cspec[upper, :], cspec[lower, :]
        cx = ci * xi
        prod_t[upper, :] = bf((cr * xr + jnp.where(first, 0.0, cx)) * weight)
        prod_t[lower, :] = bf(jnp.where(first, cx, ci * xr - cr * xi) * weight)

    sums[...] = dot(turned[0:window, :], prod_t[...])

    folded = sums[0:period, :] * env[0:period, :]
    for at in range(1, window // period):
        piece = pl.ds(at * period, period)
        folded = folded + sums[piece, :] * env[piece, :]
    folded = bf(folded * (1.0 / math.sqrt(tokens * window)))
    gts[...] = folded
    gtall[:, own_cols] = folded

    def give(peer):
        return move(4, ahead(peer), gts, gtall.at[:, own_cols])

    def taken(kind, peer):
        return move(kind, lax.rem(me - peer + n, n), gts, gtall.at[:, own_cols])

    give(across).start()
    for at in range(early):
        @pl.when((me >= side) & (across != at))
        def _():
            give(at).start()


    for peer in near:
        give(peer).start()
    send_conv(steps[EARLY:MIDDLE])

    @pl.loop(0, half // 64)
    def _(i):
        upper, lower, first, weight = parts(i)
        cr, ci = cspec[upper, :], cspec[lower, :]
        hr, hi = tspec[upper, :], tspec[lower, :]
        hc = hi * ci
        prod_g[upper, :] = bf((hr * cr + jnp.where(first, 0.0, hc)) * weight)
        prod_g[lower, :] = bf(jnp.where(first, hc, hr * ci - hi * cr) * weight)

    back_g[...] = bf(dot(turned[...], prod_g[...]))


    def forward(peer):
        return move(5, ahead(peer), gtall.at[:, columns(across)], gtall.at[:, columns(across)])

    def give_back(some):
        for at in some:
            rising = at + (me <= at).astype(jnp.int32)
            peer = jnp.where(lax.rem(mine, 2) == 0, rising, lax.rem(me + 1 + at, n))
            move(3, ahead(peer), back_g.at[block(peer), :], gi_ref.at[:, own_cols]).start()

    lower = me < side

    @pl.when(lower)
    def _():
        give_back(range(1))

    taken(4, across).wait_recv()

    @pl.when(me >= side)
    def _():
        for peer in near:
            forward(peer).start()

    for at in range(early, side):
        @pl.when((me < side) & (me != at))
        def _():
            forward(at).start()


    g_moves = [move(3, step, back_g.at[own_rows, :], gi_ref.at[:, own_cols]) for step in steps]
    @pl.when(jnp.logical_not(lower))
    def _():
        give_back(range(1))

    give_back(range(1, n - 1))
    send_conv(steps[MIDDLE:])
    gi_ref[:, own_cols] = back_g[own_rows, :]
    for peer in near:
        taken(4, peer).wait_recv()

    def unit_part(first):
        span = pl.ds(pl.multiple_of(first * width, side * width), side * width)
        return dot(gtall[:, span], ow_turned[span, :]) + dot(gtall[:, span], ow_rest[span, :])

    near_part = unit_part(base_peer)

    @pl.when(me >= side)
    def _():
        for peer in near:
            taken(5, peer).wait_recv()

    @pl.when(me < early)
    def _():
        for peer in far[1:]:
            taken(4, peer).wait_recv()

    @pl.when((me >= early) & (me < side))
    def _():
        for at in range(early):
            taken(5, at).wait_recv()
        for step in range(1, side - early):
            taken(5, early + lax.rem(me - early + step, side - early)).wait_recv()


    units[mine] = bf(near_part + unit_part(side - base_peer))
    crossing = []
    for step in sorted(range(1, m), key=lambda step: -min(step, m - step)):
        copy = pltpu.make_async_remote_copy(
            src_ref=units.at[mine], dst_ref=units.at[mine],
            send_sem=usend.at[step], recv_sem=urecv.at[step],
            device_id={"ch": others[step]}, device_id_type=MESH,
        )
        copy.start()
        crossing.append(copy)
    gow_ref[...] = dot(h_two_t, gtall[...])
    for copy in crossing:
        copy.wait_recv()
    unit = units[0].astype(jnp.float32)
    for other in range(1, m):
        unit = unit + units[other].astype(jnp.float32)
    grad_two = unit * slope_two
    narrow_two = bf(grad_two)
    grad_one = (dot(narrow_two, w2_turned) + dot(narrow_two, w2_rest)) * slope_one
    gw1_ref[...] = dot(featt_ref[...], grad_one, precision=full)
    gw2_ref[...] = dot(h_one_t, narrow_two)
    gb2_ref[...] = jnp.sum(grad_two, axis=0, keepdims=True)
    gb1_ref[...] = jnp.sum(grad_one, axis=0, keepdims=True)
    for copy in x_moves + c_moves + v_moves:
        copy.wait_send()
    for peer in near:
        give(peer).wait_send()

    give(across).wait_send()
    for at in range(early):
        @pl.when((me >= side) & (across != at))
        def _():
            give(at).wait_send()

    @pl.when(me >= side)
    def _():
        for peer in near:
            forward(peer).wait_send()

    for at in range(early, side):
        @pl.when((me < side) & (me != at))
        def _():
            forward(at).wait_send()

    for copy in crossing:
        copy.wait_send()
    for copy in g_moves:
        copy.wait()
    for copy in v_moves:
        copy.wait_recv()
    gg_ref[...] = bf(gout_ref[...].astype(jnp.float32) * conv_in[...].astype(jnp.float32))


def drain_kernel(*refs):
    count = len(refs) // 2
    store_sem = refs[-1]
    stores = [
        pltpu.make_async_copy(refs[at], refs[count + at], store_sem.at[at])
        for at in range(count)
    ]
    for copy in stores:
        copy.start()
    for copy in stores:
        copy.wait()


def exchanged(
    mesh_shape, inputs, gate_values, grad_out, first_weight, first_bias, second_weight,
    second_bias, out_weight, decay_rates, mask_lengths,
):
    n, m = mesh_shape["seq"], mesh_shape["ch"]
    rows, channels = inputs.shape
    width = channels // n
    window = SPAN * rows
    emb, units = first_weight.shape
    period = 2 * emb
    tokens = n * rows
    angles = (
        2.0 * np.pi / period
        * (np.arange(period)[:, None] * (np.arange(emb // 2)[None, :] + 1) % period)
    )
    features = np.concatenate([np.cos(angles), np.sin(angles)], axis=1).astype(np.float32)
    f32, b16 = jnp.float32, jnp.bfloat16
    outside = pl.BlockSpec(memory_space=pltpu.HBM)
    inside = pl.BlockSpec(memory_space=pltpu.VMEM)
    shape = jax.ShapeDtypeStruct
    sem = pltpu.SemaphoreType.DMA
    table = packed_table(tokens)
    staged = (
        gate_values, grad_out, first_weight, first_bias[None], second_weight,
        second_bias[None], decay_rates[None], mask_lengths[None],
        jnp.asarray(features), jnp.asarray(features.T.copy()), out_weight,
        jnp.asarray(table, dtype=b16), jnp.asarray(table.T.copy(), dtype=b16),
    )
    out_shapes = (
        shape((rows, channels), b16), shape((rows, channels), b16),
        shape((emb, units), f32), shape((1, units), f32),
        shape((units, units), f32), shape((1, units), f32),
        shape((units, channels), f32),
    )
    outs = pl.pallas_call(
        functools.partial(exchange_kernel, (n, m, rows, width, window, period)),
        out_shape=tuple(pltpu.VMEM(out.shape, out.dtype) for out in out_shapes),
        in_specs=[outside] * 14,
        out_specs=(inside,) * 7,
        scratch_shapes=[
            *[pltpu.VMEM(array.shape, array.dtype) for array in staged],
            pltpu.VMEM((channels, units), b16), pltpu.VMEM((channels, units), b16),
            pltpu.VMEM((rows, channels), b16),
            pltpu.VMEM((tokens, width), b16), pltpu.VMEM((tokens, width), b16),
            pltpu.VMEM((rows, channels), b16),
            pltpu.VMEM((window, width), b16), pltpu.VMEM((window, width), f32),
            pltpu.VMEM((tokens, width), f32), pltpu.VMEM((tokens, width), f32),
            pltpu.VMEM((tokens, width), f32),
            pltpu.VMEM((tokens, width), b16), pltpu.VMEM((tokens, width), b16),
            pltpu.VMEM((tokens, width), b16),
            pltpu.VMEM((tokens, width), b16), pltpu.VMEM((tokens, width), b16),
            pltpu.VMEM((window, width), f32),
            pltpu.VMEM((period, width), b16), pltpu.VMEM((period, channels), b16),
            pltpu.VMEM((m, period, units), b16),
            sem((6, n)), sem((6, n)), sem((m,)), sem((m,)), sem((14,)),
            pltpu.SemaphoreType.REGULAR,
        ],
        compiler_params=pltpu.CompilerParams(
            collective_id=0, has_side_effects=True, vmem_limit_bytes=VMEM_LIMIT
        ),
        name="exchange",
    )(*[pltpu.with_memory_space_constraint(array, pltpu.HBM) for array in (inputs, *staged)])
    outs = pl.pallas_call(
        drain_kernel,
        out_shape=out_shapes,
        in_specs=[inside] * 7,
        out_specs=(outside,) * 7,
        scratch_shapes=[sem((7,))],
        compiler_params=pltpu.CompilerParams(vmem_limit_bytes=DRAIN_LIMIT),
        name="drain",
    )(*outs)
    grad_in, gates, gw1, gb1, gw2, gb2, gow = outs
    return grad_in, gates, gw1, gb1[0], gw2, gb2[0], gow


def solution(mesh):
    def body(*arrays):
        rows, channels = arrays[0].shape
        count = mesh.shape["seq"]
        fits = channels == 128 * count and rows % 128 == 0 and count == 2 * SPAN
        if fits:
            return exchanged(mesh.shape, *arrays)
        return per_device(*arrays)

    in_specs = (
        P("seq", "ch"),
        P("seq", "ch"),
        P("seq", "ch"),
        P(),
        P(),
        P(),
        P(),
        P(None, "ch"),
        P("ch"),
        P("ch"),
    )
    out_specs = (P("seq", "ch"), P("seq", "ch"), P(), P(), P(), P(), P(None, "ch"))
    return jax.shard_map(
        body, mesh=mesh, in_specs=in_specs, out_specs=out_specs, check_vma=False
    )
```
